512 devices in a mesh: row: 8 (over x, core), col: 16 (over z), layer: 4 (over y).
Axes of the slice: x: 4, y: 4, z: 16, core: 2. Of those that a mesh axis runs over, the one named last changes fastest.
Arguments:
- occurrences: bfloat16 [8192, 10240], P(('row', 'col', 'layer')), may hold values from -6 to 6
- idf_weight: float32 [8192], P(('row', 'col', 'layer')), may hold values from 0.25 to 2
- pattern: int32 [64, 80], replicated, may hold values 0 or 1
Outputs:
- margin: bfloat16 [10240, 10240], P('row', 'col')
The draws below stay inside these ranges and needn't reach their ends.
All inputs are finite; a program needn't handle non-finite values.
Results may differ from the reference program's by a relative error of at most 0.0058.
Values may be sent and summed in bfloat16 or wider, within the bound.
No kernel may reach another device: no remote copies, remote signals or barrier semaphores. Data moves between devices by JAX's collectives and lax.ppermute only.
A program may use at most 64 MiB of HBM per device.

```python
import math
import jax
import jax.numpy as jnp
from jax import lax

READS = 10240
KMERS = 8192
KB = 64
RB = 80


def set_ends(array, stream_key, least, top_value):
    longest = array.shape.index(max(array.shape))
    spots = []
    for shift in (0, 1):
        where = [jax.random.randint(jax.random.fold_in(stream_key, axis), (), 0, length) for axis, length in enumerate(array.shape)]
        where[longest] = (where[longest] + shift) % array.shape[longest]
        spots.append(tuple(where))
    return array.at[spots[0]].set(least).at[spots[1]].set(top_value)


def block_levels(key, shape, shards, low, top_value):
    loudness = 1.0
    for position, blocks in shards:
        steps = jax.random.uniform(jax.random.fold_in(jax.random.fold_in(key, 6), position), (blocks,), jnp.float32, low / len(shards), top_value / len(shards))
        loudness = loudness * jnp.repeat(jnp.exp(steps), shape[position] // blocks).reshape((-1,) + (1,) * (len(shape) - 1 - position))
    return loudness


def noise(rng, shape, width, limit, split=(), dtype=jnp.bfloat16):
    values = width * jax.random.normal(rng, shape, jnp.float32)
    if split:
        values = values * block_levels(rng, shape, split, -0.22, 0.18)
    return jnp.clip(values, -limit, limit).astype(dtype)


def setup_inputs(seed: int = 0) -> dict:
    splits = jax.random.split(jax.random.key(seed), 4)
    return {
        "occurrences": noise(splits[0], (KMERS, READS), 1.0, 6.0, ((0, 512),)),
        "idf_weight": jnp.clip(jnp.exp(math.log(2.0) - 2.0794415 * jax.random.uniform(splits[1], (KMERS,), jnp.float32) ** block_levels(splits[1], (KMERS,), ((0, 512),), -0.2, 0.2)), 0.25, 2.0),
        "pattern": set_ends((jax.random.randint(splits[2], (KB, RB), 0, 2) < 1).astype(jnp.int32), jax.random.fold_in(splits[2], 1), 0, 1),
    }


def reference(occurrences, idf_weight, pattern):
    block_mask = jnp.repeat(jnp.repeat(pattern.astype(jnp.float32), 128, axis=0), 128, axis=1)
    weighted = (occurrences.astype(jnp.float32) * idf_weight[:, None] * block_mask).astype(jnp.bfloat16)
    gram = lax.dot_general(weighted, weighted, (((0,), (0,)), ((), ())), preferred_element_type=jnp.float32)
    factor = 1.0 / math.sqrt(KMERS)
    row_ids = lax.broadcasted_iota(jnp.int32, gram.shape, 0)
    col_ids = lax.broadcasted_iota(jnp.int32, gram.shape, 1)
    result = jnp.where(row_ids == col_ids, jnp.float32(0.0), gram * factor)
    return result.astype(jnp.bfloat16)
```

```python
import math

import jax
import jax.numpy as jnp
from jax import lax
from jax.experimental import pallas as pl
from jax.experimental.pallas import tpu as pltpu
from jax.sharding import Mesh
from jax.sharding import PartitionSpec as P

PLANE = ("x", "layer")
VMEM = pl.BlockSpec(memory_space=pltpu.VMEM)
SMEM = pl.BlockSpec(memory_space=pltpu.SMEM)


def order_kernel(first, step, n, near, place_ref, held_ref, near_ref, far_ref):
    start = place_ref[0]
    way = place_ref[1]
    for k in range(n):
        block = held_ref[lax.rem(start + way * k + n, n)]
        if k < near:
            near_ref[k] = block
        else:
            far_ref[n - 1 - k] = block


def gram_kernel(slots, half, place_ref, cols_ref, *refs):
    rows, (keep_ref, send_ref, acc_ref) = refs[:slots], refs[slots:]
    width = cols_ref.shape[-1]
    for s in range(slots):
        part = lax.dot_general(
            rows[s][...],
            cols_ref[:, s].reshape(-1, width),
            (((0,), (0,)), ((), ())),
            preferred_element_type=jnp.float32,
        )
        if s == 0:
            acc_ref[...] = part
        else:
            acc_ref[...] += part
    first = place_ref[0] == 0

    @pl.when(first)
    def _():
        keep_ref[...] = acc_ref[:half]
        send_ref[...] = acc_ref[half:]

    @pl.when(jnp.logical_not(first))
    def _():
        keep_ref[...] = acc_ref[half:]
        send_ref[...] = acc_ref[:half]


def body(occurrences, idf_weight, pattern):
    owned, reads = occurrences.shape
    nx, nc = lax.axis_size("x"), lax.axis_size("core")
    nz, ny = lax.axis_size("col"), lax.axis_size("layer")
    x, c = lax.axis_index("x"), lax.axis_index("core")
    z, y = lax.axis_index("col"), lax.axis_index("layer")
    factor = 1.0 / math.sqrt(owned * nx * nc * nz * ny)
    owner = lax.axis_index(("x", "core", "col", "layer"))
    flags = lax.dynamic_slice_in_dim(pattern, owner * owned // 128, 1, 0)[0]
    read_mask = jnp.repeat(flags.astype(jnp.float32), 128)
    weighted = (
        occurrences.astype(jnp.float32) * idf_weight[:, None] * read_mask[None, :]
    ).astype(jnp.bfloat16)

    width = reads // nz
    half = reads // (nx * nc * ny)
    tile = nc * half
    by_col = weighted.reshape(owned, nz, width).transpose(1, 0, 2)
    col_part = lax.all_to_all(by_col, "col", split_axis=0, concat_axis=0, tiled=True)
    by_chip = (
        weighted.reshape(owned, nx, nc, ny, half)
        .transpose(1, 3, 0, 2, 4)
        .reshape(nx * ny, owned, tile)
    )
    own = lax.all_to_all(by_chip, PLANE, split_axis=0, concat_axis=0, tiled=True)
    own = own.reshape(nx * ny * owned, tile)
    swap = [(0, 1), (1, 0)]
    other = lax.ppermute(own, "core", swap)
    ring = [(i, (i + 1) % nz) for i in range(nz)]
    ring += [(nz + i, nz + (i - 1) % nz) for i in range(nz)]
    chain_a, chain_b = [own], [other]
    for k in range(1, nz // 2):
        chain_a.append(lax.ppermute(chain_a[-1], ("core", "col"), ring))
        chain_b.append(lax.ppermute(chain_b[-1], ("core", "col"), ring))
    chain_a.append(lax.ppermute(chain_a[-1], ("core", "col"), ring))
    rows = chain_a + chain_b[1:]
    slots = len(rows)

    near = len(chain_a)
    way = 2 * c - 1
    place = jnp.stack([z, way]).astype(jnp.int32)
    near_part, far_part = pl.pallas_call(
        lambda *refs: order_kernel(0, 0, nz, near, *refs),
        out_shape=(
            jax.ShapeDtypeStruct((near, owned, width), jnp.bfloat16),
            jax.ShapeDtypeStruct((nz - near, owned, width), jnp.bfloat16),
        ),
        in_specs=[SMEM, VMEM],
        out_specs=(VMEM, VMEM),
        name="order",
    )(place, col_part)
    far_part = lax.ppermute(far_part, "core", swap)
    cols = jnp.concatenate([near_part, far_part], 0)
    chips = nx * ny
    cols = lax.all_to_all(
        jnp.broadcast_to(cols[None], (chips,) + cols.shape),
        PLANE,
        split_axis=0,
        concat_axis=0,
        tiled=True,
    )
    side = jnp.reshape(c, (1,)).astype(jnp.int32)
    keep, send = pl.pallas_call(
        lambda *refs: gram_kernel(slots, half, *refs),
        out_shape=(jax.ShapeDtypeStruct((half, width), jnp.float32),) * 2,
        in_specs=[SMEM] + [VMEM] * (1 + slots),
        out_specs=(VMEM, VMEM),
        scratch_shapes=[pltpu.VMEM((tile, width), jnp.float32)],
        compiler_params=pltpu.CompilerParams(vmem_limit_bytes=40 << 20),
        cost_estimate=pl.CostEstimate(
            flops=2 * tile * width * slots * chips * owned,
            bytes_accessed=2 * (tile + width) * slots * chips * owned,
            transcendentals=0,
        ),
        name="gram",
    )(side, cols, *rows)
    total = (keep + lax.ppermute(send, "core", swap)) * factor
    row_ids = ((x * nc + c) * ny + y) * half + lax.broadcasted_iota(jnp.int32, total.shape, 0)
    col_ids = z * width + lax.broadcasted_iota(jnp.int32, total.shape, 1)
    piece = jnp.where(row_ids == col_ids, jnp.float32(0.0), total).astype(jnp.bfloat16)
    copies = jnp.broadcast_to(piece[None], (ny,) + piece.shape)
    out = lax.all_to_all(copies, "layer", split_axis=0, concat_axis=0, tiled=True)
    return out.reshape(ny * half, width)


def solution(mesh):
    rows, cols, layers = mesh.devices.shape
    fine = Mesh(mesh.devices.reshape(rows // 2, 2, cols, layers), ("x", "core", "col", "layer"))
    owners = ("x", "core", "col", "layer")
    return jax.shard_map(
        body,
        mesh=fine,
        in_specs=(P(owners, None), P(owners), P()),
        out_specs=P(("x", "core"), "col"),
        check_vma=False,
    )
```

```python
import math

import jax
import jax.numpy as jnp
from jax import lax
from jax.experimental import pallas as pl
from jax.experimental.pallas import tpu as pltpu
from jax.sharding import Mesh
from jax.sharding import PartitionSpec as P

SMEM = pl.BlockSpec(memory_space=pltpu.SMEM)


def around(n, shift):
    return [(i, (i + shift) % n) for i in range(n)]


def spread(value, axis, n):
    return [value] + [lax.ppermute(value, axis, around(n, s)) for s in (1, 3, 2)]


SHIFTS = (0, 1, 3, 2)


def gram_kernel(half, planes, place_ref, rows_ref, *refs):
    x, y, c = place_ref[0], place_ref[1], place_ref[2]
    by_y, by_x = refs[:4], refs[4:8]
    keep_ref, send_ref, acc_ref = refs[8:]
    k = pl.program_id(0)

    @pl.when(k == 0)
    def _():
        acc_ref[...] = jnp.zeros_like(acc_ref)

    def add(right):
        left = []
        for s in SHIFTS:
            for t in SHIFTS:
                slot = lax.rem(x - s + 4, 4) * 4 + lax.rem(y - t + 4, 4)
                left.append(rows_ref[0, slot])
        acc_ref[...] += lax.dot_general(
            jnp.concatenate(left, 0),
            jnp.concatenate(right, 0),
            (((0,), (0,)), ((), ())),
            preferred_element_type=jnp.float32,
        )

    @pl.when(k < planes // 2)
    def _():
        add([by_y[j][i, 0] for i in range(4) for j in range(4)])

    @pl.when(k >= planes // 2)
    def _():
        add([by_x[i][j, 0] for i in range(4) for j in range(4)])

    last = k == planes - 1

    @pl.when(jnp.logical_and(last, c == 0))
    def _():
        keep_ref[...] = acc_ref[:half]
        send_ref[...] = acc_ref[half:]

    @pl.when(jnp.logical_and(last, c != 0))
    def _():
        keep_ref[...] = acc_ref[half:]
        send_ref[...] = acc_ref[:half]


def body(occurrences, idf_weight, pattern):
    owned, reads = occurrences.shape
    nx, nc = lax.axis_size("x"), lax.axis_size("core")
    nz, ny = lax.axis_size("col"), lax.axis_size("layer")
    x, c = lax.axis_index("x"), lax.axis_index("core")
    z, y = lax.axis_index("col"), lax.axis_index("layer")
    factor = 1.0 / math.sqrt(owned * nx * nc * nz * ny)
    owner = lax.axis_index(("x", "core", "col", "layer"))
    flags = lax.dynamic_slice_in_dim(pattern, owner * owned // 128, 1, 0)[0]
    read_mask = jnp.repeat(flags.astype(jnp.float32), 128)
    weighted = (
        occurrences.astype(jnp.float32) * idf_weight[:, None] * read_mask[None, :]
    ).astype(jnp.bfloat16)

    width = reads // nz
    half = reads // (nx * nc * ny)
    tile = nc * half
    chips = nx * ny
    by_chip = (
        weighted.reshape(owned, nx, nc, ny, half)
        .transpose(1, 3, 0, 2, 4)
        .reshape(chips, owned, tile)
    )
    own = lax.all_to_all(by_chip, ("x", "layer"), split_axis=0, concat_axis=0, tiled=True)
    own = own.reshape(chips * owned, tile)
    rows = lax.all_gather(own, "col", axis=0, tiled=True).reshape(nz, chips, owned, tile)
    by_col = weighted.reshape(owned, nz, width).transpose(1, 0, 2)
    by_col, own = lax.optimization_barrier((by_col, own))
    part = lax.all_to_all(by_col, "col", split_axis=0, concat_axis=0, tiled=True)
    upper, lower = part[: nz // 2], part[nz // 2 :]
    along_x = jnp.stack(spread(upper, "x", nx))
    along_y = jnp.stack(spread(lower, "layer", ny))
    by_y = spread(along_x, "layer", ny)
    by_x = spread(along_y, "x", nx)

    place = jnp.stack([x, y, c]).astype(jnp.int32)
    n = nz // 2
    block = (nx, 1, owned, width)
    keep, send = pl.pallas_call(
        lambda *refs: gram_kernel(half, nz, *refs),
        out_shape=(jax.ShapeDtypeStruct((half, width), jnp.float32),) * 2,
        grid=(nz,),
        in_specs=[SMEM, pl.BlockSpec((1, chips, owned, tile), lambda k: (k, 0, 0, 0))]
        + [pl.BlockSpec(block, lambda k: (0, jnp.minimum(k, n - 1), 0, 0))] * ny
        + [pl.BlockSpec(block, lambda k: (0, jnp.maximum(k - n, 0), 0, 0))] * nx,
        out_specs=(pl.BlockSpec((half, width), lambda k: (0, 0)),) * 2,
        scratch_shapes=[pltpu.VMEM((tile, width), jnp.float32)],
        compiler_params=pltpu.CompilerParams(vmem_limit_bytes=60 << 20),
        cost_estimate=pl.CostEstimate(
            flops=2 * tile * width * nz * chips * owned,
            bytes_accessed=2 * (tile + width) * nz * chips * owned,
            transcendentals=0,
        ),
        name="gram",
    )(place, rows, *by_y, *by_x)
    total = (keep + lax.ppermute(send, "core", [(0, 1), (1, 0)])) * factor
    row_ids = ((x * nc + c) * ny + y) * half + lax.broadcasted_iota(jnp.int32, total.shape, 0)
    col_ids = z * width + lax.broadcasted_iota(jnp.int32, total.shape, 1)
    piece = jnp.where(row_ids == col_ids, jnp.float32(0.0), total).astype(jnp.bfloat16)
    copies = jnp.broadcast_to(piece[None], (ny,) + piece.shape)
    out = lax.all_to_all(copies, "layer", split_axis=0, concat_axis=0, tiled=True)
    return out.reshape(ny * half, width)


def solution(mesh):
    rows, cols, layers = mesh.devices.shape
    fine = Mesh(mesh.devices.reshape(rows // 2, 2, cols, layers), ("x", "core", "col", "layer"))
    owners = ("x", "core", "col", "layer")
    return jax.shard_map(
        body,
        mesh=fine,
        in_specs=(P(owners, None), P(owners), P()),
        out_specs=P(("x", "core"), "col"),
        check_vma=False,
    )
```

```python
import math

import jax
import jax.numpy as jnp
from jax import lax
from jax.experimental import pallas as pl
from jax.experimental.pallas import tpu as pltpu
from jax.sharding import Mesh
from jax.sharding import PartitionSpec as P

VMEM = pl.BlockSpec(memory_space=pltpu.VMEM)
SMEM = pl.BlockSpec(memory_space=pltpu.SMEM)


def around(n, shift):
    return [(i, (i + shift) % n) for i in range(n)]


def spread(value, axis, n):
    return [value] + [lax.ppermute(value, axis, around(n, s)) for s in SHIFTS[1:]]


def collect(value, axis, n):
    copies = jnp.broadcast_to(value[None], (n,) + value.shape)
    return lax.all_to_all(copies, axis, split_axis=0, concat_axis=0, tiled=True)


SHIFTS = (0, 1, 3, 2)
GROUP = 4


def gram_kernel(half, steps, place_ref, rows_ref, by_y_ref, *refs):
    x, y, c = place_ref[0], place_ref[1], place_ref[2]
    by_x, (keep_ref, send_ref, acc_ref) = refs[:4], refs[4:]
    k = pl.program_id(0)

    def product(left, right):
        return lax.dot_general(
            jnp.concatenate(left, 0),
            jnp.concatenate(right, 0),
            (((0,), (0,)), ((), ())),
            preferred_element_type=jnp.float32,
        )

    def first():
        left, right = [], []
        for p in range(GROUP):
            for i in range(4):
                for j in range(4):
                    left.append(rows_ref[p, i * 4 + j])
                    right.append(by_y_ref[j, i, p])
        return product(left, right)

    def second():
        left, right = [], []
        for p in range(GROUP):
            for i, s in enumerate(SHIFTS):
                for j, t in enumerate(SHIFTS):
                    left.append(rows_ref[p, lax.rem(x - s + 4, 4) * 4 + lax.rem(y - t + 4, 4)])
                    right.append(by_x[i][j, p])
        return product(left, right)

    @pl.when(k == 0)
    def _():
        acc_ref[...] = first()

    @pl.when(jnp.logical_and(k > 0, k < steps // 2))
    def _():
        acc_ref[...] += first()

    @pl.when(k >= steps // 2)
    def _():
        acc_ref[...] += second()

    last = k == steps - 1

    @pl.when(jnp.logical_and(last, c == 0))
    def _():
        keep_ref[...] = acc_ref[:half]
        send_ref[...] = acc_ref[half:]

    @pl.when(jnp.logical_and(last, c != 0))
    def _():
        keep_ref[...] = acc_ref[half:]
        send_ref[...] = acc_ref[:half]


def finish_kernel(factor, place_ref, keep_ref, add_ref, out_ref):
    shape = keep_ref.shape
    row_ids = place_ref[0] + lax.broadcasted_iota(jnp.int32, shape, 0)
    col_ids = place_ref[1] + lax.broadcasted_iota(jnp.int32, shape, 1)
    total = (keep_ref[...] + add_ref[...]) * factor
    piece = jnp.where(row_ids == col_ids, jnp.float32(0.0), total).astype(jnp.bfloat16)
    for i in range(out_ref.shape[0]):
        out_ref[i] = piece


def body(occurrences, idf_weight, pattern):
    owned, reads = occurrences.shape
    nx, nc = lax.axis_size("x"), lax.axis_size("core")
    nz, ny = lax.axis_size("col"), lax.axis_size("layer")
    x, c = lax.axis_index("x"), lax.axis_index("core")
    z, y = lax.axis_index("col"), lax.axis_index("layer")
    factor = 1.0 / math.sqrt(owned * nx * nc * nz * ny)
    owner = lax.axis_index(("x", "core", "col", "layer"))
    flags = lax.dynamic_slice_in_dim(pattern, owner * owned // 128, 1, 0)[0]
    read_mask = jnp.repeat(flags.astype(jnp.float32), 128)
    weighted = (
        occurrences.astype(jnp.float32) * idf_weight[:, None] * read_mask[None, :]
    ).astype(jnp.bfloat16)

    width = reads // nz
    half = reads // (nx * nc * ny)
    tile = nc * half
    chips = nx * ny
    by_chip = (
        weighted.reshape(owned, nx, nc, ny, half)
        .transpose(1, 3, 0, 2, 4)
        .reshape(chips, owned, tile)
    )
    own = lax.all_to_all(by_chip, ("x", "layer"), split_axis=0, concat_axis=0, tiled=True)
    own = own.reshape(chips * owned, tile)
    rows = lax.all_gather(own, "col", axis=0, tiled=True).reshape(nz, chips, owned, tile)
    by_col = weighted.reshape(owned, nz, width).transpose(1, 0, 2)
    by_col, own = lax.optimization_barrier((by_col, own))
    part = lax.all_to_all(by_col, "col", split_axis=0, concat_axis=0, tiled=True)
    upper, lower = part[: nz // 2], part[nz // 2 :]
    along_x = collect(upper, "x", nx)
    along_y = jnp.stack(spread(lower, "layer", ny))
    along_x, along_y = lax.optimization_barrier((along_x, along_y))
    by_y = collect(along_x, "layer", ny)
    by_x = spread(along_y, "x", nx)

    place = jnp.stack([x, y, c]).astype(jnp.int32)
    steps = nz // GROUP
    n = steps // 2
    keep, send = pl.pallas_call(
        lambda *refs: gram_kernel(half, steps, *refs),
        out_shape=(jax.ShapeDtypeStruct((half, width), jnp.float32),) * 2,
        grid=(steps,),
        in_specs=[
            SMEM,
            pl.BlockSpec((GROUP, chips, owned, tile), lambda k: (k, 0, 0, 0)),
            pl.BlockSpec(
                (ny, nx, GROUP, owned, width), lambda k: (0, 0, jnp.minimum(k, n - 1), 0, 0)
            ),
        ]
        + [
            pl.BlockSpec(
                (ny, GROUP, owned, width), lambda k: (0, jnp.maximum(k - n, 0), 0, 0)
            )
        ]
        * nx,
        out_specs=(pl.BlockSpec((half, width), lambda k: (0, 0)),) * 2,
        scratch_shapes=[pltpu.VMEM((tile, width), jnp.float32)],
        compiler_params=pltpu.CompilerParams(vmem_limit_bytes=60 << 20),
        cost_estimate=pl.CostEstimate(
            flops=2 * tile * width * nz * chips * owned,
            bytes_accessed=2 * (tile + width) * nz * chips * owned,
            transcendentals=0,
        ),
        name="gram",
    )(place, rows, by_y, *by_x)
    add = lax.ppermute(send, "core", [(0, 1), (1, 0)])
    corner = jnp.stack([((x * nc + c) * ny + y) * half, z * width]).astype(jnp.int32)
    copies = pl.pallas_call(
        lambda *refs: finish_kernel(factor, *refs),
        out_shape=jax.ShapeDtypeStruct((ny, half, width), jnp.bfloat16),
        in_specs=[SMEM, VMEM, VMEM],
        out_specs=VMEM,
        compiler_params=pltpu.CompilerParams(vmem_limit_bytes=8 << 20),
        name="finish",
    )(corner, keep, add)
    out = lax.all_to_all(copies, "layer", split_axis=0, concat_axis=0, tiled=True)
    return out.reshape(ny * half, width)


def solution(mesh):
    rows, cols, layers = mesh.devices.shape
    fine = Mesh(mesh.devices.reshape(rows // 2, 2, cols, layers), ("x", "core", "col", "layer"))
    owners = ("x", "core", "col", "layer")
    return jax.shard_map(
        body,
        mesh=fine,
        in_specs=(P(owners, None), P(owners), P()),
        out_specs=P(("x", "core"), "col"),
        check_vma=False,
    )
```

```python
import math

import jax
import jax.numpy as jnp
from jax import lax
from jax.experimental import pallas as pl
from jax.experimental.pallas import tpu as pltpu
from jax.sharding import Mesh
from jax.sharding import PartitionSpec as P

VMEM = pl.BlockSpec(memory_space=pltpu.VMEM)
SMEM = pl.BlockSpec(memory_space=pltpu.SMEM)


def around(n, shift):
    return [(i, (i + shift) % n) for i in range(n)]


def spread(value, axis, n):
    return [value] + [lax.ppermute(value, axis, around(n, s)) for s in SHIFTS[1:]]


def collect(value, axis, n):
    copies = jnp.broadcast_to(value[None], (n,) + value.shape)
    return lax.all_to_all(copies, axis, split_axis=0, concat_axis=0, tiled=True)


SHIFTS = (0, 1, 3, 2)
GROUP = 4


def turn_kernel(block_ref, turned_ref):
    turned_ref[...] = block_ref[...].T


def gram_kernel(steps, place_ref, rows_ref, by_y_ref, *refs):
    by_x, (out_ref, right_ref) = refs[:4], refs[4:]
    x, y = place_ref[1], place_ref[2]
    k = pl.program_id(0)
    owned = by_y_ref.shape[3]
    width = by_y_ref.shape[4]
    chips = 16

    def product(right):
        left = jnp.concatenate([rows_ref[p] for p in range(GROUP)], 1)
        return jnp.dot(left, right, preferred_element_type=jnp.float32)

    def first():
        blocks = [
            by_y_ref[j, i, p] for p in range(GROUP) for i in range(4) for j in range(4)
        ]
        return product(jnp.concatenate(blocks, 0))

    @pl.when(k == 0)
    def _():
        out_ref[...] = first()

    @pl.when(jnp.logical_and(k > 0, k < steps // 2))
    def _():
        out_ref[...] += first()

    @pl.when(k >= steps // 2)
    def _():
        for i, s in enumerate(SHIFTS):
            for j, t in enumerate(SHIFTS):
                slot = lax.rem(x - s + 4, 4) * 4 + lax.rem(y - t + 4, 4)
                for p in range(GROUP):
                    start = pl.multiple_of(p * chips * owned + slot * owned, owned)
                    right_ref[pl.ds(start, owned), :] = by_x[i][j, p]
        out_ref[...] += product(right_ref[...])


def gram_half(place, rows, by_y, by_x, pick):
    planes, tile, depth = rows.shape
    ny, nx, _, owned, width = by_y.shape
    half = tile // 2
    steps = planes // GROUP
    n = steps // 2

    def half_of(place_ref):
        return place_ref[0] if pick == 0 else 1 - place_ref[0]

    grid_spec = pltpu.PrefetchScalarGridSpec(
        num_scalar_prefetch=1,
        grid=(steps,),
        in_specs=[
            pl.BlockSpec((GROUP, half, depth), lambda k, place_ref: (k, half_of(place_ref), 0)),
            pl.BlockSpec(
                (ny, nx, GROUP, owned, width),
                lambda k, place_ref: (0, 0, jnp.minimum(k, n - 1), 0, 0),
            ),
        ]
        + [
            pl.BlockSpec(
                (ny, GROUP, owned, width),
                lambda k, place_ref: (0, jnp.maximum(k - n, 0), 0, 0),
            )
        ]
        * nx,
        out_specs=pl.BlockSpec((half, width), lambda k, place_ref: (0, 0)),
        scratch_shapes=[pltpu.VMEM((GROUP * depth, width), jnp.bfloat16)],
    )
    return pl.pallas_call(
        lambda *refs: gram_kernel(steps, *refs),
        out_shape=jax.ShapeDtypeStruct((half, width), jnp.float32),
        grid_spec=grid_spec,
        compiler_params=pltpu.CompilerParams(vmem_limit_bytes=60 << 20),
        cost_estimate=pl.CostEstimate(
            flops=2 * half * width * planes * depth,
            bytes_accessed=2 * (half + width) * planes * depth,
            transcendentals=0,
        ),
        name="gram",
    )(place, rows, by_y, *by_x)


def finish_kernel(factor, place_ref, keep_ref, add_ref, out_ref):
    shape = keep_ref.shape
    row_ids = place_ref[0] + lax.broadcasted_iota(jnp.int32, shape, 0)
    col_ids = place_ref[1] + lax.broadcasted_iota(jnp.int32, shape, 1)
    total = (keep_ref[...] + add_ref[...]) * factor
    piece = jnp.where(row_ids == col_ids, jnp.float32(0.0), total).astype(jnp.bfloat16)
    for i in range(out_ref.shape[0]):
        out_ref[i] = piece


def body(occurrences, idf_weight, pattern):
    owned, reads = occurrences.shape
    nx, nc = lax.axis_size("x"), lax.axis_size("core")
    nz, ny = lax.axis_size("col"), lax.axis_size("layer")
    x, c = lax.axis_index("x"), lax.axis_index("core")
    z, y = lax.axis_index("col"), lax.axis_index("layer")
    factor = 1.0 / math.sqrt(owned * nx * nc * nz * ny)
    owner = lax.axis_index(("x", "core", "col", "layer"))
    flags = lax.dynamic_slice_in_dim(pattern, owner * owned // 128, 1, 0)[0]
    read_mask = jnp.repeat(flags.astype(jnp.float32), 128)
    weighted = (
        occurrences.astype(jnp.float32) * idf_weight[:, None] * read_mask[None, :]
    ).astype(jnp.bfloat16)

    width = reads // nz
    half = reads // (nx * nc * ny)
    tile = nc * half
    chips = nx * ny
    by_chip = (
        weighted.reshape(owned, nx, nc, ny, half)
        .transpose(1, 3, 0, 2, 4)
        .reshape(chips, owned, tile)
    )
    own = lax.all_to_all(by_chip, ("x", "layer"), split_axis=0, concat_axis=0, tiled=True)
    turned = pl.pallas_call(
        turn_kernel,
        out_shape=jax.ShapeDtypeStruct((tile, chips * owned), jnp.bfloat16),
        in_specs=[VMEM],
        out_specs=VMEM,
        compiler_params=pltpu.CompilerParams(vmem_limit_bytes=8 << 20),
        name="turn",
    )(own.reshape(chips * owned, tile))
    rows = lax.all_gather(turned, "col", axis=0, tiled=False)
    by_col = weighted.reshape(owned, nz, width).transpose(1, 0, 2)
    by_col, _ = lax.optimization_barrier((by_col, turned))
    part = lax.all_to_all(by_col, "col", split_axis=0, concat_axis=0, tiled=True)
    upper, lower = part[: nz // 2], part[nz // 2 :]
    along_x = collect(upper, "x", nx)
    along_y = jnp.stack(spread(lower, "layer", ny))
    along_x, along_y = lax.optimization_barrier((along_x, along_y))
    by_y = collect(along_x, "layer", ny)
    by_x = spread(along_y, "x", nx)

    place = jnp.stack([c, x, y]).astype(jnp.int32)
    send = gram_half(place, rows, by_y, by_x, 1)
    keep = gram_half(place, rows, by_y, by_x, 0)
    add = lax.ppermute(send, "core", [(0, 1), (1, 0)])
    corner = jnp.stack([((x * nc + c) * ny + y) * half, z * width]).astype(jnp.int32)
    copies = pl.pallas_call(
        lambda *refs: finish_kernel(factor, *refs),
        out_shape=jax.ShapeDtypeStruct((ny, half, width), jnp.bfloat16),
        in_specs=[SMEM, VMEM, VMEM],
        out_specs=VMEM,
        compiler_params=pltpu.CompilerParams(vmem_limit_bytes=8 << 20),
        name="finish",
    )(corner, keep, add)
    out = lax.all_to_all(copies, "layer", split_axis=0, concat_axis=0, tiled=True)
    return out.reshape(ny * half, width)


def solution(mesh):
    rows, cols, layers = mesh.devices.shape
    fine = Mesh(mesh.devices.reshape(rows // 2, 2, cols, layers), ("x", "core", "col", "layer"))
    owners = ("x", "core", "col", "layer")
    return jax.shard_map(
        body,
        mesh=fine,
        in_specs=(P(owners, None), P(owners), P()),
        out_specs=P(("x", "core"), "col"),
        check_vma=False,
    )
```

```python
import math

import jax
import jax.numpy as jnp
from jax import lax
from jax.experimental import pallas as pl
from jax.experimental.pallas import tpu as pltpu
from jax.sharding import Mesh
from jax.sharding import PartitionSpec as P

VMEM = pl.BlockSpec(memory_space=pltpu.VMEM)
SMEM = pl.BlockSpec(memory_space=pltpu.SMEM)


def around(n, shift):
    return [(i, (i + shift) % n) for i in range(n)]


def spread(value, axis, n):
    return [value] + [lax.ppermute(value, axis, around(n, s)) for s in SHIFTS[1:]]


def collect(value, axis, n):
    copies = jnp.broadcast_to(value[None], (n,) + value.shape)
    return lax.all_to_all(copies, axis, split_axis=0, concat_axis=0, tiled=True)


SHIFTS = (0, 1, 3, 2)
GROUP = 4


def weigh_kernel(owned, nz, place_ref, pattern_ref, weight_ref, block_ref, by_col_ref, by_chip_ref):
    lanes = 128
    row = place_ref[0]
    weight = weight_ref[...]
    width = by_col_ref.shape[2]
    count = width // lanes
    chips, _, tile = by_chip_ref.shape
    half = tile // 2
    strips = []
    for z in range(nz):
        parts = []
        for i in range(count):
            j = z * count + i
            flag = pattern_ref[row, j].astype(jnp.float32)
            block = block_ref[:, j * lanes : (j + 1) * lanes].astype(jnp.float32)
            parts.append((block * weight * flag).astype(jnp.bfloat16))
        strip = jnp.concatenate(parts, 1)
        by_col_ref[z] = strip
        strips.append(strip)
    for x in range(4):
        for core in range(2):
            pair = jnp.concatenate(strips[x * 4 + core * 2 : x * 4 + core * 2 + 2], 1)
            for y in range(4):
                by_chip_ref[x * 4 + y, :, core * half : (core + 1) * half] = pair[
                    :, y * half : (y + 1) * half
                ]


def gram_kernel(half, steps, place_ref, rows_ref, by_y_ref, *refs):
    x, y, c = place_ref[0], place_ref[1], place_ref[2]
    by_x, (keep_ref, send_ref, acc_ref) = refs[:4], refs[4:]
    k = pl.program_id(0)

    def product(left, right):
        return lax.dot_general(
            jnp.concatenate(left, 0),
            jnp.concatenate(right, 0),
            (((0,), (0,)), ((), ())),
            preferred_element_type=jnp.float32,
        )

    def first():
        left, right = [], []
        for p in range(GROUP):
            for i in range(4):
                for j in range(4):
                    left.append(rows_ref[p, i * 4 + j])
                    right.append(by_y_ref[j, i, p])
        return product(left, right)

    def second():
        left, right = [], []
        for p in range(GROUP):
            for i, s in enumerate(SHIFTS):
                for j, t in enumerate(SHIFTS):
                    left.append(rows_ref[p, lax.rem(x - s + 4, 4) * 4 + lax.rem(y - t + 4, 4)])
                    right.append(by_x[i][j, p])
        return product(left, right)

    @pl.when(k == 0)
    def _():
        acc_ref[...] = first()

    @pl.when(jnp.logical_and(k > 0, k < steps // 2))
    def _():
        acc_ref[...] += first()

    @pl.when(k >= steps // 2)
    def _():
        acc_ref[...] += second()

    last = k == steps - 1

    @pl.when(jnp.logical_and(last, c == 0))
    def _():
        keep_ref[...] = acc_ref[:half]
        send_ref[...] = acc_ref[half:]

    @pl.when(jnp.logical_and(last, c != 0))
    def _():
        keep_ref[...] = acc_ref[half:]
        send_ref[...] = acc_ref[:half]


def finish_kernel(factor, place_ref, keep_ref, add_ref, out_ref):
    shape = keep_ref.shape
    row_ids = place_ref[0] + pl.program_id(0) * shape[0] + lax.broadcasted_iota(jnp.int32, shape, 0)
    col_ids = place_ref[1] + lax.broadcasted_iota(jnp.int32, shape, 1)
    total = (keep_ref[...] + add_ref[...]) * factor
    piece = jnp.where(row_ids == col_ids, jnp.float32(0.0), total).astype(jnp.bfloat16)
    for i in range(out_ref.shape[0]):
        out_ref[i] = piece


def body(occurrences, idf_weight, pattern):
    owned, reads = occurrences.shape
    nx, nc = lax.axis_size("x"), lax.axis_size("core")
    nz, ny = lax.axis_size("col"), lax.axis_size("layer")
    x, c = lax.axis_index("x"), lax.axis_index("core")
    z, y = lax.axis_index("col"), lax.axis_index("layer")
    factor = 1.0 / math.sqrt(owned * nx * nc * nz * ny)
    owner = lax.axis_index(("x", "core", "col", "layer"))
    width = reads // nz
    half = reads // (nx * nc * ny)
    tile = nc * half
    chips = nx * ny
    block_row = jnp.reshape(owner * owned // 128, (1,)).astype(jnp.int32)
    by_col, by_chip = pl.pallas_call(
        lambda *refs: weigh_kernel(owned, nz, *refs),
        out_shape=(
            jax.ShapeDtypeStruct((nz, owned, width), jnp.bfloat16),
            jax.ShapeDtypeStruct((chips, owned, tile), jnp.bfloat16),
        ),
        in_specs=[SMEM, SMEM, VMEM, VMEM],
        out_specs=(VMEM, VMEM),
        compiler_params=pltpu.CompilerParams(vmem_limit_bytes=8 << 20),
        name="weigh",
    )(block_row, pattern, idf_weight.reshape(owned, 1), occurrences)
    own = lax.all_to_all(by_chip, ("x", "layer"), split_axis=0, concat_axis=0, tiled=True)
    own = own.reshape(chips * owned, tile)
    rows = lax.all_gather(own, "col", axis=0, tiled=True).reshape(nz, chips, owned, tile)
    by_col, own = lax.optimization_barrier((by_col, own))
    part = lax.all_to_all(by_col, "col", split_axis=0, concat_axis=0, tiled=True)
    upper, lower = part[: nz // 2], part[nz // 2 :]
    along_x = collect(upper, "x", nx)
    along_y = jnp.stack(spread(lower, "layer", ny))
    along_x, along_y = lax.optimization_barrier((along_x, along_y))
    by_y = collect(along_x, "layer", ny)
    by_x = spread(along_y, "x", nx)

    place = jnp.stack([x, y, c]).astype(jnp.int32)
    steps = nz // GROUP
    n = steps // 2
    keep, send = pl.pallas_call(
        lambda *refs: gram_kernel(half, steps, *refs),
        out_shape=(jax.ShapeDtypeStruct((half, width), jnp.float32),) * 2,
        grid=(steps,),
        in_specs=[
            SMEM,
            pl.BlockSpec((GROUP, chips, owned, tile), lambda k: (k, 0, 0, 0)),
            pl.BlockSpec(
                (ny, nx, GROUP, owned, width), lambda k: (0, 0, jnp.minimum(k, n - 1), 0, 0)
            ),
        ]
        + [
            pl.BlockSpec(
                (ny, GROUP, owned, width), lambda k: (0, jnp.maximum(k - n, 0), 0, 0)
            )
        ]
        * nx,
        out_specs=(VMEM, VMEM),
        scratch_shapes=[pltpu.VMEM((tile, width), jnp.float32)],
        compiler_params=pltpu.CompilerParams(vmem_limit_bytes=50 << 20),
        cost_estimate=pl.CostEstimate(
            flops=2 * tile * width * nz * chips * owned,
            bytes_accessed=2 * (tile + width) * nz * chips * owned,
            transcendentals=0,
        ),
        name="gram",
    )(place, rows, by_y, *by_x)
    add = lax.ppermute(send, "core", [(0, 1), (1, 0)])
    corner = jnp.stack([((x * nc + c) * ny + y) * half, z * width]).astype(jnp.int32)
    bands = 2
    band = pl.BlockSpec((half // bands, width), lambda k: (k, 0))
    copies = pl.pallas_call(
        lambda *refs: finish_kernel(factor, *refs),
        out_shape=jax.ShapeDtypeStruct((ny, half, width), jnp.bfloat16),
        grid=(bands,),
        in_specs=[SMEM, band, band],
        out_specs=pl.BlockSpec((ny, half // bands, width), lambda k: (0, k, 0)),
        compiler_params=pltpu.CompilerParams(vmem_limit_bytes=16 << 20),
        name="finish",
    )(corner, keep, add)
    out = lax.all_to_all(copies, "layer", split_axis=0, concat_axis=0, tiled=True)
    return out.reshape(ny * half, width)


def solution(mesh):
    rows, cols, layers = mesh.devices.shape
    fine = Mesh(mesh.devices.reshape(rows // 2, 2, cols, layers), ("x", "core", "col", "layer"))
    owners = ("x", "core", "col", "layer")
    return jax.shard_map(
        body,
        mesh=fine,
        in_specs=(P(owners, None), P(owners), P()),
        out_specs=P(("x", "core"), "col"),
        check_vma=False,
    )
```

```python
import math

import jax
import jax.numpy as jnp
from jax import lax
from jax.experimental import pallas as pl
from jax.experimental.pallas import tpu as pltpu
from jax.sharding import Mesh
from jax.sharding import PartitionSpec as P

VMEM = pl.BlockSpec(memory_space=pltpu.VMEM)
SMEM = pl.BlockSpec(memory_space=pltpu.SMEM)


def around(n, shift):
    return [(i, (i + shift) % n) for i in range(n)]


def spread(value, axis, n):
    return [value] + [lax.ppermute(value, axis, around(n, s)) for s in SHIFTS[1:]]


def collect(value, axis, n):
    copies = jnp.broadcast_to(value[None], (n,) + value.shape)
    return lax.all_to_all(copies, axis, split_axis=0, concat_axis=0, tiled=True)


SHIFTS = (0, 1, 3, 2)
GROUP = 4


def weigh_kernel(owned, nz, place_ref, pattern_ref, weight_ref, block_ref, by_col_ref, by_chip_ref):
    lanes = 128
    row = place_ref[0]
    diagonal = lax.broadcasted_iota(jnp.int32, (owned, owned), 0) == lax.broadcasted_iota(
        jnp.int32, (owned, owned), 1
    )
    spread_weight = jnp.broadcast_to(weight_ref[...], (owned, owned))
    weight = jnp.sum(jnp.where(diagonal, spread_weight, 0.0), axis=1, keepdims=True)
    width = by_col_ref.shape[2]
    count = width // lanes
    chips, _, tile = by_chip_ref.shape
    half = tile // 2
    strips = []
    for z in range(nz):
        parts = []
        for i in range(count):
            j = z * count + i
            flag = pattern_ref[row, j].astype(jnp.float32)
            block = block_ref[:, j * lanes : (j + 1) * lanes].astype(jnp.float32)
            parts.append((block * weight * flag).astype(jnp.bfloat16))
        strip = jnp.concatenate(parts, 1)
        by_col_ref[z] = strip
        strips.append(strip)
    for x in range(4):
        for core in range(2):
            pair = jnp.concatenate(strips[x * 4 + core * 2 : x * 4 + core * 2 + 2], 1)
            for y in range(4):
                by_chip_ref[x * 4 + y, :, core * half : (core + 1) * half] = pair[
                    :, y * half : (y + 1) * half
                ]


def gram_kernel(half, steps, place_ref, rows_ref, by_y_ref, *refs):
    x, y, c = place_ref[0], place_ref[1], place_ref[2]
    by_x, (keep_ref, send_ref, acc_ref) = refs[:4], refs[4:]
    k = pl.program_id(0)

    def product(left, right):
        return lax.dot_general(
            jnp.concatenate(left, 0),
            jnp.concatenate(right, 0),
            (((0,), (0,)), ((), ())),
            preferred_element_type=jnp.float32,
        )

    def first():
        left, right = [], []
        for p in range(GROUP):
            for i in range(4):
                for j in range(4):
                    left.append(rows_ref[p, i * 4 + j])
                    right.append(by_y_ref[j, i, p])
        return product(left, right)

    def second():
        left, right = [], []
        for p in range(GROUP):
            for i, s in enumerate(SHIFTS):
                for j, t in enumerate(SHIFTS):
                    left.append(rows_ref[p, lax.rem(x - s + 4, 4) * 4 + lax.rem(y - t + 4, 4)])
                    right.append(by_x[i][j, p])
        return product(left, right)

    @pl.when(k == 0)
    def _():
        acc_ref[...] = first()

    @pl.when(jnp.logical_and(k > 0, k < steps // 2))
    def _():
        acc_ref[...] += first()

    @pl.when(k >= steps // 2)
    def _():
        acc_ref[...] += second()

    last = k == steps - 1

    @pl.when(jnp.logical_and(last, c == 0))
    def _():
        keep_ref[...] = acc_ref[:half]
        send_ref[...] = acc_ref[half:]

    @pl.when(jnp.logical_and(last, c != 0))
    def _():
        keep_ref[...] = acc_ref[half:]
        send_ref[...] = acc_ref[:half]


def finish_kernel(factor, place_ref, keep_ref, add_ref, out_ref):
    shape = keep_ref.shape
    row_ids = place_ref[0] + pl.program_id(0) * shape[0] + lax.broadcasted_iota(jnp.int32, shape, 0)
    col_ids = place_ref[1] + lax.broadcasted_iota(jnp.int32, shape, 1)
    total = (keep_ref[...] + add_ref[...]) * factor
    out_ref[...] = jnp.where(row_ids == col_ids, jnp.float32(0.0), total).astype(jnp.bfloat16)


def place_kernel(order_ref, *refs):
    *piece_refs, out_ref = refs
    k = pl.program_id(0)
    for i, piece_ref in enumerate(piece_refs):

        @pl.when(k == i)
        def _():
            out_ref[0] = piece_ref[...]


def last_kernel(order_ref, held_ref, piece_ref, out_ref):
    out_ref[0] = piece_ref[...]


def assemble(order, pieces, last):
    rows, width = last.shape
    shape = jax.ShapeDtypeStruct((len(pieces) + 1, rows, width), last.dtype)

    def block(shift):
        return pl.BlockSpec((1, rows, width), lambda k, order_ref: (order_ref[k + shift], 0, 0))

    held = pl.pallas_call(
        place_kernel,
        out_shape=shape,
        grid_spec=pltpu.PrefetchScalarGridSpec(
            num_scalar_prefetch=1,
            grid=(len(pieces),),
            in_specs=[pl.BlockSpec((rows, width), lambda k, order_ref: (0, 0))] * len(pieces),
            out_specs=block(0),
        ),
        compiler_params=pltpu.CompilerParams(vmem_limit_bytes=16 << 20),
        name="place",
    )(order, *pieces)
    return pl.pallas_call(
        last_kernel,
        out_shape=shape,
        grid_spec=pltpu.PrefetchScalarGridSpec(
            num_scalar_prefetch=1,
            grid=(1,),
            in_specs=[
                pl.BlockSpec(memory_space=pl.ANY),
                pl.BlockSpec((rows, width), lambda k, order_ref: (0, 0)),
            ],
            out_specs=block(len(pieces)),
        ),
        input_output_aliases={1: 0},
        compiler_params=pltpu.CompilerParams(vmem_limit_bytes=16 << 20),
        name="last",
    )(order, held, last)


def body(occurrences, idf_weight, pattern):
    owned, reads = occurrences.shape
    nx, nc = lax.axis_size("x"), lax.axis_size("core")
    nz, ny = lax.axis_size("col"), lax.axis_size("layer")
    x, c = lax.axis_index("x"), lax.axis_index("core")
    z, y = lax.axis_index("col"), lax.axis_index("layer")
    factor = 1.0 / math.sqrt(owned * nx * nc * nz * ny)
    owner = lax.axis_index(("x", "core", "col", "layer"))
    width = reads // nz
    half = reads // (nx * nc * ny)
    tile = nc * half
    chips = nx * ny
    block_row = jnp.reshape(owner * owned // 128, (1,)).astype(jnp.int32)
    by_col, by_chip = pl.pallas_call(
        lambda *refs: weigh_kernel(owned, nz, *refs),
        out_shape=(
            jax.ShapeDtypeStruct((nz, owned, width), jnp.bfloat16),
            jax.ShapeDtypeStruct((chips, owned, tile), jnp.bfloat16),
        ),
        in_specs=[SMEM, SMEM, VMEM, VMEM],
        out_specs=(VMEM, VMEM),
        compiler_params=pltpu.CompilerParams(vmem_limit_bytes=58 << 20),
        name="weigh",
    )(block_row, pattern, idf_weight.reshape(1, owned), occurrences)
    own = lax.all_to_all(by_chip, ("x", "layer"), split_axis=0, concat_axis=0, tiled=True)
    own = own.reshape(chips * owned, tile)
    rows = lax.all_gather(own, "col", axis=0, tiled=True).reshape(nz, chips, owned, tile)
    by_col, own = lax.optimization_barrier((by_col, own))
    part = lax.all_to_all(by_col, "col", split_axis=0, concat_axis=0, tiled=True)
    upper, lower = part[: nz // 2], part[nz // 2 :]
    along_x = collect(upper, "x", nx)
    along_y = jnp.stack(spread(lower, "layer", ny))
    along_x, along_y = lax.optimization_barrier((along_x, along_y))
    by_y = collect(along_x, "layer", ny)
    by_x = spread(along_y, "x", nx)

    place = jnp.stack([x, y, c]).astype(jnp.int32)
    steps = nz // GROUP
    n = steps // 2
    keep, send = pl.pallas_call(
        lambda *refs: gram_kernel(half, steps, *refs),
        out_shape=(jax.ShapeDtypeStruct((half, width), jnp.float32),) * 2,
        grid=(steps,),
        in_specs=[
            SMEM,
            pl.BlockSpec((GROUP, chips, owned, tile), lambda k: (k, 0, 0, 0)),
            pl.BlockSpec(
                (ny, nx, GROUP, owned, width), lambda k: (0, 0, jnp.minimum(k, n - 1), 0, 0)
            ),
        ]
        + [
            pl.BlockSpec(
                (ny, GROUP, owned, width), lambda k: (0, jnp.maximum(k - n, 0), 0, 0)
            )
        ]
        * nx,
        out_specs=(VMEM, VMEM),
        scratch_shapes=[pltpu.VMEM((tile, width), jnp.float32)],
        compiler_params=pltpu.CompilerParams(vmem_limit_bytes=50 << 20),
        cost_estimate=pl.CostEstimate(
            flops=2 * tile * width * nz * chips * owned,
            bytes_accessed=2 * (tile + width) * nz * chips * owned,
            transcendentals=0,
        ),
        name="gram",
    )(place, rows, by_y, *by_x)
    add = lax.ppermute(send, "core", [(0, 1), (1, 0)])
    corner = jnp.stack([((x * nc + c) * ny + y) * half, z * width]).astype(jnp.int32)
    bands = 2
    band = pl.BlockSpec((half // bands, width), lambda k: (k, 0))
    piece = pl.pallas_call(
        lambda *refs: finish_kernel(factor, *refs),
        out_shape=jax.ShapeDtypeStruct((half, width), jnp.bfloat16),
        grid=(bands,),
        in_specs=[SMEM, band, band],
        out_specs=band,
        compiler_params=pltpu.CompilerParams(vmem_limit_bytes=16 << 20),
        name="finish",
    )(corner, keep, add)
    up = around(ny, 1)
    down = around(ny, ny - 1)
    ways = [up + [(ny + i, ny + j) for i, j in down], down + [(ny + i, ny + j) for i, j in up]]
    ahead = lax.ppermute(piece, ("core", "layer"), ways[0])
    behind = lax.ppermute(piece, ("core", "layer"), ways[1])
    across = lax.ppermute(ahead, ("core", "layer"), ways[0])
    way = 1 - 2 * c
    order = jnp.stack([y, (y - way + ny) % ny, (y + way + ny) % ny, (y + 2) % ny])
    out = assemble(order.astype(jnp.int32), [piece, ahead, behind], across)
    return out.reshape(ny * half, width)


def solution(mesh):
    rows, cols, layers = mesh.devices.shape
    fine = Mesh(mesh.devices.reshape(rows // 2, 2, cols, layers), ("x", "core", "col", "layer"))
    owners = ("x", "core", "col", "layer")
    return jax.shard_map(
        body,
        mesh=fine,
        in_specs=(P(owners, None), P(owners), P()),
        out_specs=P(("x", "core"), "col"),
        check_vma=False,
    )
```

```python
import math

import jax
import jax.numpy as jnp
from jax import lax
from jax.experimental import pallas as pl
from jax.experimental.pallas import tpu as pltpu
from jax.sharding import Mesh
from jax.sharding import PartitionSpec as P

VMEM = pl.BlockSpec(memory_space=pltpu.VMEM)
SMEM = pl.BlockSpec(memory_space=pltpu.SMEM)


def around(n, shift):
    return [(i, (i + shift) % n) for i in range(n)]


def spread(value, axis, n):
    return [value] + [lax.ppermute(value, axis, around(n, s)) for s in SHIFTS[1:]]


def relay(values, axes, sizes):
    groups, ways = [], []
    for axis, n in zip(axes, sizes):
        if axis == "x":
            groups.append(("x", "core"))
            spot = lambda core, i: 2 * i + core
        else:
            groups.append(("core", axis))
            spot = lambda core, i, n=n: core * n + i
        ways.append(
            [
                [(spot(core, i), spot(core, j)) for core in (0, 1) for i, j in around(n, way * (1 - 2 * core))]
                for way in (1, -1)
            ]
        )
    ahead = [lax.ppermute(v, g, w[0]) for v, g, w in zip(values, groups, ways)]
    behind = [lax.ppermute(v, g, w[1]) for v, g, w in zip(values, groups, ways)]
    across = [lax.ppermute(v, g, w[0]) for v, g, w in zip(ahead, groups, ways)]
    return [list(blocks) for blocks in zip(values, ahead, behind, across)]


def collect(value, axis, n):
    copies = jnp.broadcast_to(value[None], (n,) + value.shape)
    return lax.all_to_all(copies, axis, split_axis=0, concat_axis=0, tiled=True)


SHIFTS = (0, 1, 3, 2)
GROUP = 4


def weigh_kernel(owned, nz, place_ref, pattern_ref, weight_ref, block_ref, by_col_ref, by_chip_ref):
    lanes = 128
    row = place_ref[0]
    diagonal = lax.broadcasted_iota(jnp.int32, (owned, owned), 0) == lax.broadcasted_iota(
        jnp.int32, (owned, owned), 1
    )
    spread_weight = jnp.broadcast_to(weight_ref[...], (owned, owned))
    weight = jnp.sum(jnp.where(diagonal, spread_weight, 0.0), axis=1, keepdims=True)
    width = by_col_ref.shape[2]
    count = width // lanes
    chips, _, tile = by_chip_ref.shape
    half = tile // 2
    strips = []
    for z in range(nz):
        parts = []
        for i in range(count):
            j = z * count + i
            flag = pattern_ref[row, j].astype(jnp.float32)
            block = block_ref[:, j * lanes : (j + 1) * lanes].astype(jnp.float32)
            parts.append((block * weight * flag).astype(jnp.bfloat16))
        strip = jnp.concatenate(parts, 1)
        by_col_ref[z] = strip
        strips.append(strip)
    for x in range(4):
        for core in range(2):
            pair = jnp.concatenate(strips[x * 4 + core * 2 : x * 4 + core * 2 + 2], 1)
            for y in range(4):
                by_chip_ref[x * 4 + y, :, core * half : (core + 1) * half] = pair[
                    :, y * half : (y + 1) * half
                ]


def gram_kernel(half, steps, place_ref, rows_ref, *refs):
    x, y, c = place_ref[0], place_ref[1], place_ref[2]
    by_y, by_x, (keep_ref, send_ref, acc_ref) = refs[:4], refs[4:8], refs[8:]
    k = pl.program_id(0)
    way = 1 - 2 * c
    offsets = (0, way, -way, 2)

    def before(position, offset):
        return lax.rem(position - offset + 4, 4)

    def product(left, right):
        return lax.dot_general(
            jnp.concatenate(left, 0),
            jnp.concatenate(right, 0),
            (((0,), (0,)), ((), ())),
            preferred_element_type=jnp.float32,
        )

    def first():
        left, right = [], []
        for p in range(GROUP):
            for i in range(4):
                for j in range(4):
                    left.append(rows_ref[p, i * 4 + before(y, offsets[j])])
                    right.append(by_y[j][i, p])
        return product(left, right)

    def second():
        left, right = [], []
        for p in range(GROUP):
            for i in range(4):
                for j in range(4):
                    left.append(
                        rows_ref[p, before(x, offsets[i]) * 4 + before(y, SHIFTS[j])]
                    )
                    right.append(by_x[i][j, p])
        return product(left, right)

    @pl.when(k == 0)
    def _():
        acc_ref[...] = first()

    @pl.when(jnp.logical_and(k > 0, k < steps // 2))
    def _():
        acc_ref[...] += first()

    @pl.when(k >= steps // 2)
    def _():
        acc_ref[...] += second()

    last = k == steps - 1

    @pl.when(jnp.logical_and(last, c == 0))
    def _():
        keep_ref[...] = acc_ref[:half]
        send_ref[...] = acc_ref[half:]

    @pl.when(jnp.logical_and(last, c != 0))
    def _():
        keep_ref[...] = acc_ref[half:]
        send_ref[...] = acc_ref[:half]


def finish_kernel(factor, corner_ref, keep_ref, add_ref, out_ref, held_ref, sems):
    bands = held_ref.shape[0]
    rows, width = held_ref.shape[1:]
    copies = [
        pltpu.make_async_copy(keep_ref.at[pl.ds(i * rows, rows)], held_ref.at[i], sems.at[i])
        for i in range(bands)
    ]
    for copy in copies:
        copy.start()
    for i, copy in enumerate(copies):
        row_ids = corner_ref[0] + i * rows + lax.broadcasted_iota(jnp.int32, (rows, width), 0)
        col_ids = corner_ref[1] + lax.broadcasted_iota(jnp.int32, (rows, width), 1)
        copy.wait()
        total = (held_ref[i] + add_ref[i * rows : (i + 1) * rows]) * factor
        out_ref[i * rows : (i + 1) * rows] = jnp.where(
            row_ids == col_ids, jnp.float32(0.0), total
        ).astype(jnp.bfloat16)


def place_kernel(own_ref, ahead_ref, behind_ref, out_ref, sems):
    y = lax.axis_index("layer")
    way = 1 - 2 * lax.axis_index("core")
    copies = []
    for i, (ref, offset) in enumerate(((own_ref, 0), (ahead_ref, way), (behind_ref, -way))):
        slot = lax.rem(y - offset + 4, 4)
        copies.append(pltpu.make_async_copy(ref, out_ref.at[slot], sems.at[i]))
    for copy in copies:
        copy.start()
    for copy in copies:
        copy.wait()


def last_kernel(held_ref, across_ref, out_ref, sem):
    slot = lax.rem(lax.axis_index("layer") + 2, 4)
    copy = pltpu.make_async_copy(across_ref, out_ref.at[slot], sem)
    copy.start()
    copy.wait()


def assemble(own, ahead, behind, across):
    shape = jax.ShapeDtypeStruct((4,) + own.shape, own.dtype)
    params = pltpu.CompilerParams(vmem_limit_bytes=8 << 20)
    anywhere = pl.BlockSpec(memory_space=pl.ANY)
    held = pl.pallas_call(
        place_kernel,
        out_shape=shape,
        in_specs=[VMEM] * 3,
        out_specs=anywhere,
        scratch_shapes=[pltpu.SemaphoreType.DMA((3,))],
        compiler_params=params,
        name="place",
    )(own, ahead, behind)
    return pl.pallas_call(
        last_kernel,
        out_shape=shape,
        in_specs=[anywhere, VMEM],
        out_specs=anywhere,
        scratch_shapes=[pltpu.SemaphoreType.DMA],
        input_output_aliases={0: 0},
        compiler_params=params,
        name="last",
    )(held, across)


def body(occurrences, idf_weight, pattern):
    owned, reads = occurrences.shape
    nx, nc = lax.axis_size("x"), lax.axis_size("core")
    nz, ny = lax.axis_size("col"), lax.axis_size("layer")
    x, c = lax.axis_index("x"), lax.axis_index("core")
    z, y = lax.axis_index("col"), lax.axis_index("layer")
    factor = 1.0 / math.sqrt(owned * nx * nc * nz * ny)
    owner = lax.axis_index(("x", "core", "col", "layer"))
    width = reads // nz
    half = reads // (nx * nc * ny)
    tile = nc * half
    chips = nx * ny
    block_row = jnp.reshape(owner * owned // 128, (1,)).astype(jnp.int32)
    by_col, by_chip = pl.pallas_call(
        lambda *refs: weigh_kernel(owned, nz, *refs),
        out_shape=(
            jax.ShapeDtypeStruct((nz, owned, width), jnp.bfloat16),
            jax.ShapeDtypeStruct((chips, owned, tile), jnp.bfloat16),
        ),
        in_specs=[SMEM, SMEM, VMEM, VMEM],
        out_specs=(VMEM, VMEM),
        compiler_params=pltpu.CompilerParams(vmem_limit_bytes=58 << 20),
        name="weigh",
    )(block_row, pattern, idf_weight.reshape(1, owned), occurrences)
    own = lax.all_to_all(by_chip, ("x", "layer"), split_axis=0, concat_axis=0, tiled=True)
    own = own.reshape(chips * owned, tile)
    rows = lax.all_gather(own, "col", axis=0, tiled=True).reshape(nz, chips, owned, tile)
    by_col, own = lax.optimization_barrier((by_col, own))
    part = lax.all_to_all(by_col, "col", split_axis=0, concat_axis=0, tiled=True)
    upper, lower = part[: nz // 2], part[nz // 2 :]
    along_x = collect(upper, "x", nx)
    along_y = jnp.stack(spread(lower, "layer", ny))
    along_x, along_y = lax.optimization_barrier((along_x, along_y))
    by_x, by_y = relay([along_y, along_x], ["x", "layer"], [nx, ny])

    place = jnp.stack([x, y, c]).astype(jnp.int32)
    steps = nz // GROUP
    n = steps // 2
    keep, send = pl.pallas_call(
        lambda *refs: gram_kernel(half, steps, *refs),
        out_shape=(jax.ShapeDtypeStruct((half, width), jnp.float32),) * 2,
        grid=(steps,),
        in_specs=[
            SMEM,
            pl.BlockSpec((GROUP, chips, owned, tile), lambda k: (k, 0, 0, 0)),
        ]
        + [
            pl.BlockSpec((nx, GROUP, owned, width), lambda k: (0, jnp.minimum(k, n - 1), 0, 0))
        ]
        * ny
        + [
            pl.BlockSpec((ny, GROUP, owned, width), lambda k: (0, jnp.maximum(k - n, 0), 0, 0))
        ]
        * nx,
        out_specs=(VMEM, VMEM),
        scratch_shapes=[pltpu.VMEM((tile, width), jnp.float32)],
        compiler_params=pltpu.CompilerParams(vmem_limit_bytes=52846592),
        cost_estimate=pl.CostEstimate(
            flops=2 * tile * width * nz * chips * owned,
            bytes_accessed=2 * (tile + width) * nz * chips * owned,
            transcendentals=0,
        ),
        name="gram",
    )(place, rows, *by_y, *by_x)
    add = lax.ppermute(send, "core", [(0, 1), (1, 0)])
    corner = jnp.stack([((x * nc + c) * ny + y) * half, z * width]).astype(jnp.int32)
    bands = 2
    piece = pl.pallas_call(
        lambda *refs: finish_kernel(factor, *refs),
        out_shape=jax.ShapeDtypeStruct((half, width), jnp.bfloat16),
        in_specs=[SMEM, pl.BlockSpec(memory_space=pl.ANY), VMEM],
        out_specs=VMEM,
        scratch_shapes=[
            pltpu.VMEM((bands, half // bands, width), jnp.float32),
            pltpu.SemaphoreType.DMA((bands,)),
        ],
        compiler_params=pltpu.CompilerParams(vmem_limit_bytes=16 << 20),
        name="finish",
    )(corner, keep, add)
    (pieces,) = relay([piece], ["layer"], [ny])
    return assemble(*pieces).reshape(ny * half, width)


def solution(mesh):
    rows, cols, layers = mesh.devices.shape
    fine = Mesh(mesh.devices.reshape(rows // 2, 2, cols, layers), ("x", "core", "col", "layer"))
    owners = ("x", "core", "col", "layer")
    return jax.shard_map(
        body,
        mesh=fine,
        in_specs=(P(owners, None), P(owners), P()),
        out_specs=P(("x", "core"), "col"),
        check_vma=False,
    )
```

```python
import math

import jax
import jax.numpy as jnp
from jax import lax
from jax.experimental import pallas as pl
from jax.experimental.pallas import tpu as pltpu
from jax.sharding import Mesh
from jax.sharding import PartitionSpec as P

VMEM = pl.BlockSpec(memory_space=pltpu.VMEM)
SMEM = pl.BlockSpec(memory_space=pltpu.SMEM)


def around(n, shift):
    return [(i, (i + shift) % n) for i in range(n)]


def spread(value, axis, n):
    return [value] + [lax.ppermute(value, axis, around(n, s)) for s in SHIFTS[1:]]


def ways_of(axis, n):
    group = ("x", "core") if axis == "x" else ("core", axis)

    def spot(core, i):
        return 2 * i + core if axis == "x" else core * n + i

    ways = []
    for way in (1, -1):
        pairs = []
        for core in (0, 1):
            pairs += [(spot(core, i), spot(core, j)) for i, j in around(n, way * (1 - 2 * core))]
        ways.append(pairs)
    return group, ways


def relay(values, axes, sizes):
    plans = [ways_of(axis, n) for axis, n in zip(axes, sizes)]
    ahead = [lax.ppermute(v, g, w[0]) for v, (g, w) in zip(values, plans)]
    behind = [lax.ppermute(v, g, w[1]) for v, (g, w) in zip(values, plans)]
    across = [lax.ppermute(v, g, w[0]) for v, (g, w) in zip(ahead, plans)]
    return [list(blocks) for blocks in zip(values, ahead, behind, across)]


def collect(value, axis, n):
    copies = jnp.broadcast_to(value[None], (n,) + value.shape)
    return lax.all_to_all(copies, axis, split_axis=0, concat_axis=0, tiled=True)


SHIFTS = (0, 1, 3, 2)
GROUP = 4


def weigh_kernel(owned, nz, place_ref, pattern_ref, weight_ref, block_ref, by_col_ref, by_chip_ref):
    lanes = 128
    row = place_ref[0]
    diagonal = lax.broadcasted_iota(jnp.int32, (owned, owned), 0) == lax.broadcasted_iota(
        jnp.int32, (owned, owned), 1
    )
    spread_weight = jnp.broadcast_to(weight_ref[...], (owned, owned))
    weight = jnp.sum(jnp.where(diagonal, spread_weight, 0.0), axis=1, keepdims=True)
    width = by_col_ref.shape[2]
    count = width // lanes
    chips, _, tile = by_chip_ref.shape
    half = tile // 2
    strips = []
    for z in range(nz):
        parts = []
        for i in range(count):
            j = z * count + i
            flag = pattern_ref[row, j].astype(jnp.float32)
            block = block_ref[:, j * lanes : (j + 1) * lanes].astype(jnp.float32)
            parts.append((block * weight * flag).astype(jnp.bfloat16))
        strip = jnp.concatenate(parts, 1)
        by_col_ref[z] = strip
        strips.append(strip)
    for x in range(4):
        for core in range(2):
            pair = jnp.concatenate(strips[x * 4 + core * 2 : x * 4 + core * 2 + 2], 1)
            for y in range(4):
                by_chip_ref[x * 4 + y, :, core * half : (core + 1) * half] = pair[
                    :, y * half : (y + 1) * half
                ]


def gram_kernel(half, steps, place_ref, rows_ref, *refs):
    x, y, c = place_ref[0], place_ref[1], place_ref[2]
    by_y, by_x, (keep_ref, send_ref, acc_ref) = refs[:4], refs[4:8], refs[8:]
    k = pl.program_id(0)
    way = 1 - 2 * c
    offsets = (0, way, -way, 2)

    def before(position, offset):
        return lax.rem(position - offset + 4, 4)

    def product(left, right):
        return lax.dot_general(
            jnp.concatenate(left, 0),
            jnp.concatenate(right, 0),
            (((0,), (0,)), ((), ())),
            preferred_element_type=jnp.float32,
        )

    def first():
        left, right = [], []
        for p in range(GROUP):
            for i in range(4):
                for j in range(4):
                    left.append(rows_ref[p, i * 4 + before(y, offsets[j])])
                    right.append(by_y[j][i, p])
        return product(left, right)

    def second():
        left, right = [], []
        for p in range(GROUP):
            for i in range(4):
                for j in range(4):
                    left.append(
                        rows_ref[p, before(x, offsets[i]) * 4 + before(y, SHIFTS[j])]
                    )
                    right.append(by_x[i][j, p])
        return product(left, right)

    @pl.when(k == 0)
    def _():
        acc_ref[...] = first()

    @pl.when(jnp.logical_and(k > 0, k < steps // 2))
    def _():
        acc_ref[...] += first()

    @pl.when(k >= steps // 2)
    def _():
        acc_ref[...] += second()

    last = k == steps - 1

    @pl.when(jnp.logical_and(last, c == 0))
    def _():
        keep_ref[...] = acc_ref[:half]
        send_ref[...] = acc_ref[half:]

    @pl.when(jnp.logical_and(last, c != 0))
    def _():
        keep_ref[...] = acc_ref[half:]
        send_ref[...] = acc_ref[:half]


def place_kernel(own_ref, ahead_ref, behind_ref, out_ref, sems):
    y = lax.axis_index("layer")
    way = 1 - 2 * lax.axis_index("core")
    copies = []
    for i, (ref, offset) in enumerate(((own_ref, 0), (ahead_ref, way), (behind_ref, -way))):
        slot = lax.rem(y - offset + 4, 4)
        copies.append(pltpu.make_async_copy(ref, out_ref.at[slot], sems.at[i]))
    for copy in copies:
        copy.start()
    for copy in copies:
        copy.wait()


def last_kernel(held_ref, across_ref, out_ref, sem):
    slot = lax.rem(lax.axis_index("layer") + 2, 4)
    copy = pltpu.make_async_copy(across_ref, out_ref.at[slot], sem)
    copy.start()
    copy.wait()


def assemble(own, ahead, behind, across):
    shape = jax.ShapeDtypeStruct((4,) + own.shape, own.dtype)
    params = pltpu.CompilerParams(vmem_limit_bytes=8 << 20)
    anywhere = pl.BlockSpec(memory_space=pl.ANY)
    held = pl.pallas_call(
        place_kernel,
        out_shape=shape,
        in_specs=[VMEM] * 3,
        out_specs=anywhere,
        scratch_shapes=[pltpu.SemaphoreType.DMA((3,))],
        compiler_params=params,
        name="place",
    )(own, ahead, behind)
    return pl.pallas_call(
        last_kernel,
        out_shape=shape,
        in_specs=[anywhere, VMEM],
        out_specs=anywhere,
        scratch_shapes=[pltpu.SemaphoreType.DMA],
        input_output_aliases={0: 0},
        compiler_params=params,
        name="last",
    )(held, across)


def body(occurrences, idf_weight, pattern):
    owned, reads = occurrences.shape
    nx, nc = lax.axis_size("x"), lax.axis_size("core")
    nz, ny = lax.axis_size("col"), lax.axis_size("layer")
    x, c = lax.axis_index("x"), lax.axis_index("core")
    z, y = lax.axis_index("col"), lax.axis_index("layer")
    factor = 1.0 / math.sqrt(owned * nx * nc * nz * ny)
    owner = lax.axis_index(("x", "core", "col", "layer"))
    width = reads // nz
    half = reads // (nx * nc * ny)
    tile = nc * half
    chips = nx * ny
    block_row = jnp.reshape(owner * owned // 128, (1,)).astype(jnp.int32)
    by_col, by_chip = pl.pallas_call(
        lambda *refs: weigh_kernel(owned, nz, *refs),
        out_shape=(
            jax.ShapeDtypeStruct((nz, owned, width), jnp.bfloat16),
            jax.ShapeDtypeStruct((chips, owned, tile), jnp.bfloat16),
        ),
        in_specs=[SMEM, SMEM, VMEM, VMEM],
        out_specs=(VMEM, VMEM),
        compiler_params=pltpu.CompilerParams(vmem_limit_bytes=58 << 20),
        name="weigh",
    )(block_row, pattern, idf_weight.reshape(1, owned), occurrences)
    own = lax.all_to_all(by_chip, ("x", "layer"), split_axis=0, concat_axis=0, tiled=True)
    own = own.reshape(chips * owned, tile)
    rows = lax.all_gather(own, "col", axis=0, tiled=True).reshape(nz, chips, owned, tile)
    by_col, own = lax.optimization_barrier((by_col, own))
    part = lax.all_to_all(by_col, "col", split_axis=0, concat_axis=0, tiled=True)
    upper, lower = part[: nz // 2], part[nz // 2 :]
    along_x = collect(upper, "x", nx)
    along_y = jnp.stack(spread(lower, "layer", ny))
    along_x, along_y = lax.optimization_barrier((along_x, along_y))
    by_x, by_y = relay([along_y, along_x], ["x", "layer"], [nx, ny])

    place = jnp.stack([x, y, c]).astype(jnp.int32)
    steps = nz // GROUP
    n = steps // 2
    keep, send = pl.pallas_call(
        lambda *refs: gram_kernel(half, steps, *refs),
        out_shape=(jax.ShapeDtypeStruct((half, width), jnp.float32),) * 2,
        grid=(steps,),
        in_specs=[
            SMEM,
            pl.BlockSpec((GROUP, chips, owned, tile), lambda k: (k, 0, 0, 0)),
        ]
        + [
            pl.BlockSpec((nx, GROUP, owned, width), lambda k: (0, jnp.minimum(k, n - 1), 0, 0))
        ]
        * ny
        + [
            pl.BlockSpec((ny, GROUP, owned, width), lambda k: (0, jnp.maximum(k - n, 0), 0, 0))
        ]
        * nx,
        out_specs=(VMEM, VMEM),
        scratch_shapes=[pltpu.VMEM((tile, width), jnp.float32)],
        compiler_params=pltpu.CompilerParams(vmem_limit_bytes=52846592),
        cost_estimate=pl.CostEstimate(
            flops=2 * tile * width * nz * chips * owned,
            bytes_accessed=2 * (tile + width) * nz * chips * owned,
            transcendentals=0,
        ),
        name="gram",
    )(place, rows, *by_y, *by_x)
    add = lax.ppermute(send, "core", [(0, 1), (1, 0)])
    total = (keep + add) * factor
    row_ids = ((x * nc + c) * ny + y) * half + lax.broadcasted_iota(jnp.int32, total.shape, 0)
    col_ids = z * width + lax.broadcasted_iota(jnp.int32, total.shape, 1)
    piece = jnp.where(row_ids == col_ids, jnp.float32(0.0), total).astype(jnp.bfloat16)
    ((own, ahead, behind, across),) = relay([piece], ["layer"], [ny])
    return assemble(own, ahead, behind, across).reshape(ny * half, width)


def solution(mesh):
    rows, cols, layers = mesh.devices.shape
    fine = Mesh(mesh.devices.reshape(rows // 2, 2, cols, layers), ("x", "core", "col", "layer"))
    owners = ("x", "core", "col", "layer")
    return jax.shard_map(
        body,
        mesh=fine,
        in_specs=(P(owners, None), P(owners), P()),
        out_specs=P(("x", "core"), "col"),
        check_vma=False,
    )
```

```python
import math

import jax
import jax.numpy as jnp
from jax import lax
from jax.experimental import pallas as pl
from jax.experimental.pallas import tpu as pltpu
from jax.sharding import Mesh
from jax.sharding import PartitionSpec as P

VMEM = pl.BlockSpec(memory_space=pltpu.VMEM)
SMEM = pl.BlockSpec(memory_space=pltpu.SMEM)


def around(n, shift):
    return [(i, (i + shift) % n) for i in range(n)]


def spread(value, axis, n):
    return [value] + [lax.ppermute(value, axis, around(n, s)) for s in SHIFTS[1:]]


def ways_of(axis, n):
    group = ("x", "core") if axis == "x" else ("core", axis)

    def spot(core, i):
        return 2 * i + core if axis == "x" else core * n + i

    ways = []
    for way in (1, -1):
        pairs = []
        for core in (0, 1):
            pairs += [(spot(core, i), spot(core, j)) for i, j in around(n, way * (1 - 2 * core))]
        ways.append(pairs)
    return group, ways


def relay(values, axes, sizes):
    plans = [ways_of(axis, n) for axis, n in zip(axes, sizes)]
    ahead = [lax.ppermute(v, g, w[0]) for v, (g, w) in zip(values, plans)]
    behind = [lax.ppermute(v, g, w[1]) for v, (g, w) in zip(values, plans)]
    across = [lax.ppermute(v, g, w[0]) for v, (g, w) in zip(ahead, plans)]
    return [list(blocks) for blocks in zip(values, ahead, behind, across)]


def collect(value, axis, n):
    copies = jnp.broadcast_to(value[None], (n,) + value.shape)
    return lax.all_to_all(copies, axis, split_axis=0, concat_axis=0, tiled=True)


SHIFTS = (0, 1, 3, 2)
GROUP = 8


def strips(nz, place_ref, pattern_ref, weight_ref, block_ref):
    lanes = 128
    owned, reads = block_ref.shape
    row = place_ref[0]
    diagonal = lax.broadcasted_iota(jnp.int32, (owned, owned), 0) == lax.broadcasted_iota(
        jnp.int32, (owned, owned), 1
    )
    spread_weight = jnp.broadcast_to(weight_ref[...], (owned, owned))
    weight = jnp.sum(jnp.where(diagonal, spread_weight, 0.0), axis=1, keepdims=True)
    count = reads // nz // lanes
    for z in range(nz):
        parts = []
        for j in range(z * count, (z + 1) * count):
            flag = pattern_ref[row, j].astype(jnp.float32)
            block = block_ref[:, j * lanes : (j + 1) * lanes].astype(jnp.float32)
            parts.append((block * weight * flag).astype(jnp.bfloat16))
        yield jnp.concatenate(parts, 1)


def cols_kernel(nz, place_ref, pattern_ref, weight_ref, block_ref, out_ref):
    for z, strip in enumerate(strips(nz, place_ref, pattern_ref, weight_ref, block_ref)):
        out_ref[z] = strip


def chips_kernel(nz, place_ref, pattern_ref, weight_ref, block_ref, out_ref):
    half = out_ref.shape[2] // 2
    held = []
    for z, strip in enumerate(strips(nz, place_ref, pattern_ref, weight_ref, block_ref)):
        held.append(strip)
        if z % 2 == 0:
            continue
        pair = jnp.concatenate(held[-2:], 1)
        x, core = z // 4, z // 2 % 2
        for y in range(4):
            out_ref[x * 4 + y, :, core * half : (core + 1) * half] = pair[
                :, y * half : (y + 1) * half
            ]


def gram_kernel(half, steps, place_ref, rows_ref, *refs):
    x, y, c = place_ref[0], place_ref[1], place_ref[2]
    by_y, by_x, (keep_ref, send_ref, acc_ref) = refs[:4], refs[4:8], refs[8:]
    k = pl.program_id(0)
    way = 1 - 2 * c
    offsets = (0, way, -way, 2)

    def before(position, offset):
        return lax.rem(position - offset + 4, 4)

    def product(left, right):
        return lax.dot_general(
            jnp.concatenate(left, 0),
            jnp.concatenate(right, 0),
            (((0,), (0,)), ((), ())),
            preferred_element_type=jnp.float32,
        )

    def first():
        left, right = [], []
        for p in range(GROUP):
            for i in range(4):
                for j in range(4):
                    left.append(rows_ref[p, i * 4 + before(y, offsets[j])])
                    right.append(by_y[j][i, p])
        return product(left, right)

    def second():
        left, right = [], []
        for p in range(GROUP):
            for i in range(4):
                for j in range(4):
                    left.append(
                        rows_ref[p, before(x, offsets[i]) * 4 + before(y, SHIFTS[j])]
                    )
                    right.append(by_x[i][j, p])
        return product(left, right)

    @pl.when(k == 0)
    def _():
        acc_ref[...] = first()

    @pl.when(jnp.logical_and(k > 0, k < steps // 2))
    def _():
        acc_ref[...] += first()

    @pl.when(k >= steps // 2)
    def _():
        acc_ref[...] += second()

    last = k == steps - 1

    @pl.when(jnp.logical_and(last, c == 0))
    def _():
        keep_ref[...] = acc_ref[:half]
        send_ref[...] = acc_ref[half:]

    @pl.when(jnp.logical_and(last, c != 0))
    def _():
        keep_ref[...] = acc_ref[half:]
        send_ref[...] = acc_ref[:half]


def place_kernel(own_ref, ahead_ref, behind_ref, out_ref, sems):
    y = lax.axis_index("layer")
    way = 1 - 2 * lax.axis_index("core")
    copies = []
    for i, (ref, offset) in enumerate(((own_ref, 0), (ahead_ref, way), (behind_ref, -way))):
        slot = lax.rem(y - offset + 4, 4)
        copies.append(pltpu.make_async_copy(ref, out_ref.at[slot], sems.at[i]))
    for copy in copies:
        copy.start()
    for copy in copies:
        copy.wait()


def last_kernel(held_ref, across_ref, out_ref, sem):
    slot = lax.rem(lax.axis_index("layer") + 2, 4)
    copy = pltpu.make_async_copy(across_ref, out_ref.at[slot], sem)
    copy.start()
    copy.wait()


def assemble(own, ahead, behind, across):
    shape = jax.ShapeDtypeStruct((4,) + own.shape, own.dtype)
    params = pltpu.CompilerParams(vmem_limit_bytes=8 << 20)
    anywhere = pl.BlockSpec(memory_space=pl.ANY)
    held = pl.pallas_call(
        place_kernel,
        out_shape=shape,
        in_specs=[VMEM] * 3,
        out_specs=anywhere,
        scratch_shapes=[pltpu.SemaphoreType.DMA((3,))],
        compiler_params=params,
        name="place",
    )(own, ahead, behind)
    return pl.pallas_call(
        last_kernel,
        out_shape=shape,
        in_specs=[anywhere, VMEM],
        out_specs=anywhere,
        scratch_shapes=[pltpu.SemaphoreType.DMA],
        input_output_aliases={0: 0},
        compiler_params=params,
        name="last",
    )(held, across)


def body(occurrences, idf_weight, pattern):
    owned, reads = occurrences.shape
    nx, nc = lax.axis_size("x"), lax.axis_size("core")
    nz, ny = lax.axis_size("col"), lax.axis_size("layer")
    x, c = lax.axis_index("x"), lax.axis_index("core")
    z, y = lax.axis_index("col"), lax.axis_index("layer")
    factor = 1.0 / math.sqrt(owned * nx * nc * nz * ny)
    owner = lax.axis_index(("x", "core", "col", "layer"))
    width = reads // nz
    half = reads // (nx * nc * ny)
    tile = nc * half
    chips = nx * ny
    block_row = jnp.reshape(owner * owned // 128, (1,)).astype(jnp.int32)
    by_col, by_chip = [
        pl.pallas_call(
            lambda *refs, kernel=kernel: kernel(nz, *refs),
            out_shape=jax.ShapeDtypeStruct((count, owned, across), jnp.bfloat16),
            in_specs=[SMEM, SMEM, VMEM, VMEM],
            out_specs=VMEM,
            compiler_params=pltpu.CompilerParams(vmem_limit_bytes=58 << 20),
            cost_estimate=pl.CostEstimate(
                flops=4 * owned * reads, bytes_accessed=4 * owned * reads, transcendentals=0
            ),
            name=name,
        )(block_row, pattern, idf_weight.reshape(1, owned), occurrences)
        for kernel, count, across, name in (
            (cols_kernel, nz, width, "weigh_cols"),
            (chips_kernel, chips, tile, "weigh_chips"),
        )
    ]
    own = lax.all_to_all(by_chip, ("x", "layer"), split_axis=0, concat_axis=0, tiled=True)
    own = own.reshape(chips * owned, tile)
    by_col, own = lax.optimization_barrier((by_col, own))
    rows = lax.all_gather(own, "col", axis=0, tiled=True).reshape(nz, chips, owned, tile)
    part = lax.all_to_all(by_col, "col", split_axis=0, concat_axis=0, tiled=True)
    upper, lower = part[: nz // 2], part[nz // 2 :]
    along_x = collect(upper, "x", nx)
    along_y = jnp.stack(spread(lower, "layer", ny))
    along_x, along_y = lax.optimization_barrier((along_x, along_y))
    by_x, by_y = relay([along_y, along_x], ["x", "layer"], [nx, ny])

    place = jnp.stack([x, y, c]).astype(jnp.int32)
    steps = nz // GROUP
    n = steps // 2
    keep, send = pl.pallas_call(
        lambda *refs: gram_kernel(half, steps, *refs),
        out_shape=(jax.ShapeDtypeStruct((half, width), jnp.float32),) * 2,
        grid=(steps,),
        in_specs=[
            SMEM,
            pl.BlockSpec((GROUP, chips, owned, tile), lambda k: (k, 0, 0, 0)),
        ]
        + [
            pl.BlockSpec((nx, GROUP, owned, width), lambda k: (0, jnp.minimum(k, n - 1), 0, 0))
        ]
        * ny
        + [
            pl.BlockSpec((ny, GROUP, owned, width), lambda k: (0, jnp.maximum(k - n, 0), 0, 0))
        ]
        * nx,
        out_specs=(VMEM, VMEM),
        scratch_shapes=[pltpu.VMEM((tile, width), jnp.float32)],
        compiler_params=pltpu.CompilerParams(vmem_limit_bytes=52846592),
        cost_estimate=pl.CostEstimate(
            flops=2 * tile * width * nz * chips * owned,
            bytes_accessed=2 * (tile + width) * nz * chips * owned,
            transcendentals=0,
        ),
        name="gram",
    )(place, rows, *by_y, *by_x)
    add = lax.ppermute(send, "core", [(0, 1), (1, 0)])
    total = (keep + add) * factor
    row_ids = ((x * nc + c) * ny + y) * half + lax.broadcasted_iota(jnp.int32, total.shape, 0)
    col_ids = z * width + lax.broadcasted_iota(jnp.int32, total.shape, 1)
    piece = jnp.where(row_ids == col_ids, jnp.float32(0.0), total).astype(jnp.bfloat16)
    ((own, ahead, behind, across),) = relay([piece], ["layer"], [ny])
    return assemble(own, ahead, behind, across).reshape(ny * half, width)


def solution(mesh):
    rows, cols, layers = mesh.devices.shape
    fine = Mesh(mesh.devices.reshape(rows // 2, 2, cols, layers), ("x", "core", "col", "layer"))
    owners = ("x", "core", "col", "layer")
    return jax.shard_map(
        body,
        mesh=fine,
        in_specs=(P(owners, None), P(owners), P()),
        out_specs=P(("x", "core"), "col"),
        check_vma=False,
    )
```

```python
import math

import jax
import jax.numpy as jnp
from jax import lax
from jax.experimental import pallas as pl
from jax.experimental.pallas import tpu as pltpu
from jax.sharding import Mesh
from jax.sharding import PartitionSpec as P

VMEM = pl.BlockSpec(memory_space=pltpu.VMEM)
SMEM = pl.BlockSpec(memory_space=pltpu.SMEM)


def around(n, shift):
    return [(i, (i + shift) % n) for i in range(n)]


def relay(values, axes, sizes):
    groups, ways = [], []
    for axis, n in zip(axes, sizes):
        if axis == "x":
            groups.append(("x", "core"))
            spot = lambda core, i: 2 * i + core
        else:
            groups.append(("core", axis))
            spot = lambda core, i, n=n: core * n + i
        ways.append(
            [
                [(spot(core, i), spot(core, j)) for core in (0, 1) for i, j in around(n, way * (1 - 2 * core))]
                for way in (1, -1)
            ]
        )
    ahead = [lax.ppermute(v, g, w[0]) for v, g, w in zip(values, groups, ways)]
    behind = [lax.ppermute(v, g, w[1]) for v, g, w in zip(values, groups, ways)]
    across = [lax.ppermute(v, g, w[0]) for v, g, w in zip(ahead, groups, ways)]
    return [list(blocks) for blocks in zip(values, ahead, behind, across)]


GROUP = 4


def weigh_kernel(owned, nz, place_ref, pattern_ref, weight_ref, block_ref, by_col_ref, by_chip_ref):
    lanes = 128
    row = place_ref[0]
    diagonal = lax.broadcasted_iota(jnp.int32, (owned, owned), 0) == lax.broadcasted_iota(
        jnp.int32, (owned, owned), 1
    )
    spread_weight = jnp.broadcast_to(weight_ref[...], (owned, owned))
    weight = jnp.sum(jnp.where(diagonal, spread_weight, 0.0), axis=1, keepdims=True)
    width = by_col_ref.shape[2]
    count = width // lanes
    chips, _, tile = by_chip_ref.shape
    half = tile // 2
    strips = []
    for z in range(nz):
        parts = []
        for i in range(count):
            j = z * count + i
            flag = pattern_ref[row, j].astype(jnp.float32)
            block = block_ref[:, j * lanes : (j + 1) * lanes].astype(jnp.float32)
            parts.append((block * weight * flag).astype(jnp.bfloat16))
        strip = jnp.concatenate(parts, 1)
        by_col_ref[z] = strip
        strips.append(strip)
    for x in range(4):
        for core in range(2):
            pair = jnp.concatenate(strips[x * 4 + core * 2 : x * 4 + core * 2 + 2], 1)
            for y in range(4):
                by_chip_ref[x * 4 + y, :, core * half : (core + 1) * half] = pair[
                    :, y * half : (y + 1) * half
                ]


def gram_kernel(half, steps, place_ref, rows_ref, *refs):
    x, y, c = place_ref[0], place_ref[1], place_ref[2]
    by_y, by_x, (keep_ref, send_ref, acc_ref) = refs[:4], refs[4:8], refs[8:]
    k = pl.program_id(0)
    way = 1 - 2 * c
    offsets = (0, way, -way, 2)

    def before(position, offset):
        return lax.rem(position - offset + 4, 4)

    def product(left, right):
        return lax.dot_general(
            jnp.concatenate(left, 0),
            jnp.concatenate(right, 0),
            (((0,), (0,)), ((), ())),
            preferred_element_type=jnp.float32,
        )

    def part(pick):
        left, right = [], []
        for p in range(GROUP):
            for i in range(4):
                for j in range(4):
                    left.append(rows_ref[p, before(x, offsets[i]) * 4 + before(y, offsets[j])])
                    right.append(pick(i, j, p))
        return product(left, right)

    def first():
        return part(lambda i, j, p: by_y[j][i, p])

    def second():
        return part(lambda i, j, p: by_x[i][j, p])

    @pl.when(k == 0)
    def _():
        acc_ref[...] = first()

    @pl.when(jnp.logical_and(k > 0, k < steps // 2))
    def _():
        acc_ref[...] += first()

    @pl.when(k >= steps // 2)
    def _():
        acc_ref[...] += second()

    last = k == steps - 1

    @pl.when(jnp.logical_and(last, c == 0))
    def _():
        keep_ref[...] = acc_ref[:half]
        send_ref[...] = acc_ref[half:]

    @pl.when(jnp.logical_and(last, c != 0))
    def _():
        keep_ref[...] = acc_ref[half:]
        send_ref[...] = acc_ref[:half]


def finish_kernel(factor, corner_ref, keep_ref, add_ref, out_ref, held_ref, sems):
    bands = held_ref.shape[0]
    rows, width = held_ref.shape[1:]
    copies = [
        pltpu.make_async_copy(keep_ref.at[pl.ds(i * rows, rows)], held_ref.at[i], sems.at[i])
        for i in range(bands)
    ]
    for copy in copies:
        copy.start()
    for i, copy in enumerate(copies):
        row_ids = corner_ref[0] + i * rows + lax.broadcasted_iota(jnp.int32, (rows, width), 0)
        col_ids = corner_ref[1] + lax.broadcasted_iota(jnp.int32, (rows, width), 1)
        copy.wait()
        total = (held_ref[i] + add_ref[i * rows : (i + 1) * rows]) * factor
        out_ref[i * rows : (i + 1) * rows] = jnp.where(
            row_ids == col_ids, jnp.float32(0.0), total
        ).astype(jnp.bfloat16)


def place_kernel(own_ref, ahead_ref, behind_ref, out_ref, sems):
    y = lax.axis_index("layer")
    way = 1 - 2 * lax.axis_index("core")
    copies = []
    for i, (ref, offset) in enumerate(((own_ref, 0), (ahead_ref, way), (behind_ref, -way))):
        slot = lax.rem(y - offset + 4, 4)
        copies.append(pltpu.make_async_copy(ref, out_ref.at[slot], sems.at[i]))
    for copy in copies:
        copy.start()
    for copy in copies:
        copy.wait()


def last_kernel(held_ref, across_ref, out_ref, sem):
    slot = lax.rem(lax.axis_index("layer") + 2, 4)
    copy = pltpu.make_async_copy(across_ref, out_ref.at[slot], sem)
    copy.start()
    copy.wait()


def assemble(own, ahead, behind, across):
    shape = jax.ShapeDtypeStruct((4,) + own.shape, own.dtype)
    params = pltpu.CompilerParams(vmem_limit_bytes=8 << 20)
    anywhere = pl.BlockSpec(memory_space=pl.ANY)
    held = pl.pallas_call(
        place_kernel,
        out_shape=shape,
        in_specs=[VMEM] * 3,
        out_specs=anywhere,
        scratch_shapes=[pltpu.SemaphoreType.DMA((3,))],
        compiler_params=params,
        name="place",
    )(own, ahead, behind)
    return pl.pallas_call(
        last_kernel,
        out_shape=shape,
        in_specs=[anywhere, VMEM],
        out_specs=anywhere,
        scratch_shapes=[pltpu.SemaphoreType.DMA],
        input_output_aliases={0: 0},
        compiler_params=params,
        name="last",
    )(held, across)


def body(occurrences, idf_weight, pattern):
    owned, reads = occurrences.shape
    nx, nc = lax.axis_size("x"), lax.axis_size("core")
    nz, ny = lax.axis_size("col"), lax.axis_size("layer")
    x, c = lax.axis_index("x"), lax.axis_index("core")
    z, y = lax.axis_index("col"), lax.axis_index("layer")
    factor = 1.0 / math.sqrt(owned * nx * nc * nz * ny)
    owner = lax.axis_index(("x", "core", "col", "layer"))
    width = reads // nz
    half = reads // (nx * nc * ny)
    tile = nc * half
    chips = nx * ny
    block_row = jnp.reshape(owner * owned // 128, (1,)).astype(jnp.int32)
    by_col, by_chip = pl.pallas_call(
        lambda *refs: weigh_kernel(owned, nz, *refs),
        out_shape=(
            jax.ShapeDtypeStruct((nz, owned, width), jnp.bfloat16),
            jax.ShapeDtypeStruct((chips, owned, tile), jnp.bfloat16),
        ),
        in_specs=[SMEM, SMEM, VMEM, VMEM],
        out_specs=(VMEM, VMEM),
        compiler_params=pltpu.CompilerParams(vmem_limit_bytes=58 << 20),
        name="weigh",
    )(block_row, pattern, idf_weight.reshape(1, owned), occurrences)
    own = lax.all_to_all(by_chip, ("x", "layer"), split_axis=0, concat_axis=0, tiled=True)
    own = own.reshape(chips * owned, tile)
    rows = lax.all_gather(own, "col", axis=0, tiled=True).reshape(nz, chips, owned, tile)
    by_col, own = lax.optimization_barrier((by_col, own))
    part = lax.all_to_all(by_col, "col", split_axis=0, concat_axis=0, tiled=True)
    upper, lower = part[: nz // 2], part[nz // 2 :]
    along_x, along_y = map(jnp.stack, relay([upper, lower], ["x", "layer"], [nx, ny]))
    along_x, along_y = lax.optimization_barrier((along_x, along_y))
    by_x, by_y = relay([along_y, along_x], ["x", "layer"], [nx, ny])

    place = jnp.stack([x, y, c]).astype(jnp.int32)
    steps = nz // GROUP
    n = steps // 2
    keep, send = pl.pallas_call(
        lambda *refs: gram_kernel(half, steps, *refs),
        out_shape=(jax.ShapeDtypeStruct((half, width), jnp.float32),) * 2,
        grid=(steps,),
        in_specs=[
            SMEM,
            pl.BlockSpec((GROUP, chips, owned, tile), lambda k: (k, 0, 0, 0)),
        ]
        + [
            pl.BlockSpec((nx, GROUP, owned, width), lambda k: (0, jnp.minimum(k, n - 1), 0, 0))
        ]
        * ny
        + [
            pl.BlockSpec((ny, GROUP, owned, width), lambda k: (0, jnp.maximum(k - n, 0), 0, 0))
        ]
        * nx,
        out_specs=(VMEM, VMEM),
        scratch_shapes=[pltpu.VMEM((tile, width), jnp.float32)],
        compiler_params=pltpu.CompilerParams(vmem_limit_bytes=52846592),
        cost_estimate=pl.CostEstimate(
            flops=2 * tile * width * nz * chips * owned,
            bytes_accessed=2 * (tile + width) * nz * chips * owned,
            transcendentals=0,
        ),
        name="gram",
    )(place, rows, *by_y, *by_x)
    add = lax.ppermute(send, "core", [(0, 1), (1, 0)])
    corner = jnp.stack([((x * nc + c) * ny + y) * half, z * width]).astype(jnp.int32)
    bands = 2
    piece = pl.pallas_call(
        lambda *refs: finish_kernel(factor, *refs),
        out_shape=jax.ShapeDtypeStruct((half, width), jnp.bfloat16),
        in_specs=[SMEM, pl.BlockSpec(memory_space=pl.ANY), VMEM],
        out_specs=VMEM,
        scratch_shapes=[
            pltpu.VMEM((bands, half // bands, width), jnp.float32),
            pltpu.SemaphoreType.DMA((bands,)),
        ],
        compiler_params=pltpu.CompilerParams(vmem_limit_bytes=16 << 20),
        name="finish",
    )(corner, keep, add)
    (pieces,) = relay([piece], ["layer"], [ny])
    return assemble(*pieces).reshape(ny * half, width)


def solution(mesh):
    rows, cols, layers = mesh.devices.shape
    fine = Mesh(mesh.devices.reshape(rows // 2, 2, cols, layers), ("x", "core", "col", "layer"))
    owners = ("x", "core", "col", "layer")
    return jax.shard_map(
        body,
        mesh=fine,
        in_specs=(P(owners, None), P(owners), P()),
        out_specs=P(("x", "core"), "col"),
        check_vma=False,
    )
```

```python
import math

import jax
import jax.numpy as jnp
from jax import lax
from jax.experimental import pallas as pl
from jax.experimental.pallas import tpu as pltpu
from jax.sharding import Mesh
from jax.sharding import PartitionSpec as P

VMEM = pl.BlockSpec(memory_space=pltpu.VMEM)
SMEM = pl.BlockSpec(memory_space=pltpu.SMEM)


def around(n, shift):
    return [(i, (i + shift) % n) for i in range(n)]


def spread(value, axis, n):
    return [value] + [lax.ppermute(value, axis, around(n, s)) for s in SHIFTS[1:]]


def relay(values, axes, sizes):
    groups, ways = [], []
    for axis, n in zip(axes, sizes):
        if axis == "x":
            groups.append(("x", "core"))
            spot = lambda core, i: 2 * i + core
        else:
            groups.append(("core", axis))
            spot = lambda core, i, n=n: core * n + i
        ways.append(
            [
                [(spot(core, i), spot(core, j)) for core in (0, 1) for i, j in around(n, way * (1 - 2 * core))]
                for way in (1, -1)
            ]
        )
    ahead = [lax.ppermute(v, g, w[0]) for v, g, w in zip(values, groups, ways)]
    behind = [lax.ppermute(v, g, w[1]) for v, g, w in zip(values, groups, ways)]
    across = [lax.ppermute(v, g, w[0]) for v, g, w in zip(ahead, groups, ways)]
    return [list(blocks) for blocks in zip(values, ahead, behind, across)]


def collect(value, axis, n):
    copies = jnp.broadcast_to(value[None], (n,) + value.shape)
    return lax.all_to_all(copies, axis, split_axis=0, concat_axis=0, tiled=True)


SHIFTS = (0, 1, 3, 2)
GROUP = 4


def weigh_kernel(
    owned, nz, place_ref, pattern_hbm, weight_ref, block_hbm, by_col_ref, by_chip_ref, pattern_ref, block_ref, sems
):
    lanes = 128
    whole = place_ref[0]
    row = lax.rem(whole, 8)
    first = pl.multiple_of(whole - row, 8)
    flags = pltpu.make_async_copy(pattern_hbm.at[pl.ds(first, 8)], pattern_ref, sems.at[4])
    flags.start()
    span = block_hbm.shape[1] // 4
    loads = []
    for i in range(4):
        part = pl.ds(i * span, span)
        loads.append(pltpu.make_async_copy(block_hbm.at[:, part], block_ref.at[:, part], sems.at[i]))
        loads[-1].start()
    diagonal = lax.broadcasted_iota(jnp.int32, (owned, owned), 0) == lax.broadcasted_iota(
        jnp.int32, (owned, owned), 1
    )
    spread_weight = jnp.broadcast_to(weight_ref[...], (owned, owned))
    weight = jnp.sum(jnp.where(diagonal, spread_weight, 0.0), axis=1, keepdims=True)
    width = by_col_ref.shape[2]
    count = width // lanes
    chips, _, tile = by_chip_ref.shape
    half = tile // 2
    strips = []
    flags.wait()
    for z in range(nz):
        if z % (nz // 4) == 0:
            loads[z // (nz // 4)].wait()
        parts = []
        for i in range(count):
            j = z * count + i
            flag = pattern_ref[row, j].astype(jnp.float32)
            block = block_ref[:, j * lanes : (j + 1) * lanes].astype(jnp.float32)
            parts.append((block * weight * flag).astype(jnp.bfloat16))
        strip = jnp.concatenate(parts, 1)
        by_col_ref[z] = strip
        strips.append(strip)
    for x in range(4):
        for core in range(2):
            pair = jnp.concatenate(strips[x * 4 + core * 2 : x * 4 + core * 2 + 2], 1)
            for y in range(4):
                by_chip_ref[x * 4 + y, :, core * half : (core + 1) * half] = pair[
                    :, y * half : (y + 1) * half
                ]


def gram_kernel(half, steps, place_ref, rows_ref, *refs):
    x, y, c = place_ref[0], place_ref[1], place_ref[2]
    by_y, by_x, (keep_ref, send_ref, acc_ref) = refs[:4], refs[4:8], refs[8:]
    k = pl.program_id(0)
    way = 1 - 2 * c
    offsets = (0, way, -way, 2)

    def before(position, offset):
        return lax.rem(position - offset + 4, 4)

    def product(left, right):
        return lax.dot_general(
            jnp.concatenate(left, 0),
            jnp.concatenate(right, 0),
            (((0,), (0,)), ((), ())),
            preferred_element_type=jnp.float32,
        )

    def first():
        left, right = [], []
        for p in range(GROUP):
            for i in range(4):
                for j in range(4):
                    left.append(rows_ref[p, i * 4 + before(y, offsets[j])])
                    right.append(by_y[j][i, p])
        return product(left, right)

    def second():
        left, right = [], []
        for p in range(GROUP):
            for i in range(4):
                for j in range(4):
                    left.append(
                        rows_ref[p, before(x, offsets[i]) * 4 + before(y, SHIFTS[j])]
                    )
                    right.append(by_x[i][j, p])
        return product(left, right)

    @pl.when(k == 0)
    def _():
        acc_ref[...] = first()

    @pl.when(jnp.logical_and(k > 0, k < steps // 2))
    def _():
        acc_ref[...] += first()

    @pl.when(k >= steps // 2)
    def _():
        acc_ref[...] += second()

    last = k == steps - 1

    @pl.when(jnp.logical_and(last, c == 0))
    def _():
        keep_ref[...] = acc_ref[:half]
        send_ref[...] = acc_ref[half:]

    @pl.when(jnp.logical_and(last, c != 0))
    def _():
        keep_ref[...] = acc_ref[half:]
        send_ref[...] = acc_ref[:half]


def finish_kernel(factor, corner_ref, keep_ref, add_ref, out_ref, held_ref, sems):
    bands = held_ref.shape[0]
    rows, width = held_ref.shape[1:]
    copies = [
        pltpu.make_async_copy(keep_ref.at[pl.ds(i * rows, rows)], held_ref.at[i], sems.at[i])
        for i in range(bands)
    ]
    for copy in copies:
        copy.start()
    for i, copy in enumerate(copies):
        row_ids = corner_ref[0] + i * rows + lax.broadcasted_iota(jnp.int32, (rows, width), 0)
        col_ids = corner_ref[1] + lax.broadcasted_iota(jnp.int32, (rows, width), 1)
        copy.wait()
        total = (held_ref[i] + add_ref[i * rows : (i + 1) * rows]) * factor
        out_ref[i * rows : (i + 1) * rows] = jnp.where(
            row_ids == col_ids, jnp.float32(0.0), total
        ).astype(jnp.bfloat16)


def place_kernel(own_ref, ahead_ref, behind_ref, out_ref, sems):
    y = lax.axis_index("layer")
    way = 1 - 2 * lax.axis_index("core")
    copies = []
    for i, (ref, offset) in enumerate(((own_ref, 0), (ahead_ref, way), (behind_ref, -way))):
        slot = lax.rem(y - offset + 4, 4)
        copies.append(pltpu.make_async_copy(ref, out_ref.at[slot], sems.at[i]))
    for copy in copies:
        copy.start()
    for copy in copies:
        copy.wait()


def last_kernel(held_ref, across_ref, out_ref, sem):
    slot = lax.rem(lax.axis_index("layer") + 2, 4)
    copy = pltpu.make_async_copy(across_ref, out_ref.at[slot], sem)
    copy.start()
    copy.wait()


def assemble(own, ahead, behind, across):
    shape = jax.ShapeDtypeStruct((4,) + own.shape, own.dtype)
    params = pltpu.CompilerParams(vmem_limit_bytes=8 << 20)
    anywhere = pl.BlockSpec(memory_space=pl.ANY)
    held = pl.pallas_call(
        place_kernel,
        out_shape=shape,
        in_specs=[VMEM] * 3,
        out_specs=anywhere,
        scratch_shapes=[pltpu.SemaphoreType.DMA((3,))],
        compiler_params=params,
        name="place",
    )(own, ahead, behind)
    return pl.pallas_call(
        last_kernel,
        out_shape=shape,
        in_specs=[anywhere, VMEM],
        out_specs=anywhere,
        scratch_shapes=[pltpu.SemaphoreType.DMA],
        input_output_aliases={0: 0},
        compiler_params=params,
        name="last",
    )(held, across)


def body(occurrences, idf_weight, pattern):
    owned, reads = occurrences.shape
    nx, nc = lax.axis_size("x"), lax.axis_size("core")
    nz, ny = lax.axis_size("col"), lax.axis_size("layer")
    x, c = lax.axis_index("x"), lax.axis_index("core")
    z, y = lax.axis_index("col"), lax.axis_index("layer")
    factor = 1.0 / math.sqrt(owned * nx * nc * nz * ny)
    owner = lax.axis_index(("x", "core", "col", "layer"))
    width = reads // nz
    half = reads // (nx * nc * ny)
    tile = nc * half
    chips = nx * ny
    block_row = jnp.reshape(owner * owned // 128, (1,)).astype(jnp.int32)
    by_col, by_chip = pl.pallas_call(
        lambda *refs: weigh_kernel(owned, nz, *refs),
        out_shape=(
            jax.ShapeDtypeStruct((nz, owned, width), jnp.bfloat16),
            jax.ShapeDtypeStruct((chips, owned, tile), jnp.bfloat16),
        ),
        in_specs=[SMEM, pl.BlockSpec(memory_space=pl.ANY), VMEM, pl.BlockSpec(memory_space=pl.ANY)],
        out_specs=(VMEM, VMEM),
        scratch_shapes=[
            pltpu.SMEM((8, pattern.shape[1]), jnp.int32),
            pltpu.VMEM((owned, reads), jnp.bfloat16),
            pltpu.SemaphoreType.DMA((5,)),
        ],
        compiler_params=pltpu.CompilerParams(vmem_limit_bytes=58 << 20),
        name="weigh",
    )(block_row, pattern, idf_weight.reshape(1, owned), occurrences)
    own = lax.all_to_all(by_chip, ("x", "layer"), split_axis=0, concat_axis=0, tiled=True)
    own = own.reshape(chips * owned, tile)
    rows = lax.all_gather(own, "col", axis=0, tiled=True).reshape(nz, chips, owned, tile)
    by_col, own = lax.optimization_barrier((by_col, own))
    part = lax.all_to_all(by_col, "col", split_axis=0, concat_axis=0, tiled=True)
    upper, lower = part[: nz // 2], part[nz // 2 :]
    along_x = collect(upper, "x", nx)
    along_y = jnp.stack(spread(lower, "layer", ny))
    along_x, along_y = lax.optimization_barrier((along_x, along_y))
    by_x, by_y = relay([along_y, along_x], ["x", "layer"], [nx, ny])

    place = jnp.stack([x, y, c]).astype(jnp.int32)
    steps = nz // GROUP
    n = steps // 2
    keep, send = pl.pallas_call(
        lambda *refs: gram_kernel(half, steps, *refs),
        out_shape=(jax.ShapeDtypeStruct((half, width), jnp.float32),) * 2,
        grid=(steps,),
        in_specs=[
            SMEM,
            pl.BlockSpec((GROUP, chips, owned, tile), lambda k: (k, 0, 0, 0)),
        ]
        + [
            pl.BlockSpec((nx, GROUP, owned, width), lambda k: (0, jnp.minimum(k, n - 1), 0, 0))
        ]
        * ny
        + [
            pl.BlockSpec((ny, GROUP, owned, width), lambda k: (0, jnp.maximum(k - n, 0), 0, 0))
        ]
        * nx,
        out_specs=(VMEM, VMEM),
        scratch_shapes=[pltpu.VMEM((tile, width), jnp.float32)],
        compiler_params=pltpu.CompilerParams(vmem_limit_bytes=52846592),
        cost_estimate=pl.CostEstimate(
            flops=2 * tile * width * nz * chips * owned,
            bytes_accessed=2 * (tile + width) * nz * chips * owned,
            transcendentals=0,
        ),
        name="gram",
    )(place, rows, *by_y, *by_x)
    add = lax.ppermute(send, "core", [(0, 1), (1, 0)])
    corner = jnp.stack([((x * nc + c) * ny + y) * half, z * width]).astype(jnp.int32)
    bands = 2
    piece = pl.pallas_call(
        lambda *refs: finish_kernel(factor, *refs),
        out_shape=jax.ShapeDtypeStruct((half, width), jnp.bfloat16),
        in_specs=[SMEM, pl.BlockSpec(memory_space=pl.ANY), VMEM],
        out_specs=VMEM,
        scratch_shapes=[
            pltpu.VMEM((bands, half // bands, width), jnp.float32),
            pltpu.SemaphoreType.DMA((bands,)),
        ],
        compiler_params=pltpu.CompilerParams(vmem_limit_bytes=16 << 20),
        name="finish",
    )(corner, keep, add)
    (pieces,) = relay([piece], ["layer"], [ny])
    return assemble(*pieces).reshape(ny * half, width)


def solution(mesh):
    rows, cols, layers = mesh.devices.shape
    fine = Mesh(mesh.devices.reshape(rows // 2, 2, cols, layers), ("x", "core", "col", "layer"))
    owners = ("x", "core", "col", "layer")
    return jax.shard_map(
        body,
        mesh=fine,
        in_specs=(P(owners, None), P(owners), P()),
        out_specs=P(("x", "core"), "col"),
        check_vma=False,
    )
```

```python
import math

import jax
import jax.numpy as jnp
from jax import lax
from jax.experimental import pallas as pl
from jax.experimental.pallas import tpu as pltpu
from jax.sharding import Mesh
from jax.sharding import PartitionSpec as P

VMEM = pl.BlockSpec(memory_space=pltpu.VMEM)
SMEM = pl.BlockSpec(memory_space=pltpu.SMEM)


def around(n, shift):
    return [(i, (i + shift) % n) for i in range(n)]


def spread(value, axis, n):
    return [value] + [lax.ppermute(value, axis, around(n, s)) for s in SHIFTS[1:]]


def relay(values, axes, sizes):
    groups, ways = [], []
    for axis, n in zip(axes, sizes):
        if axis == "x":
            groups.append(("x", "core"))
            spot = lambda core, i: 2 * i + core
        else:
            groups.append(("core", axis))
            spot = lambda core, i, n=n: core * n + i
        ways.append(
            [
                [(spot(core, i), spot(core, j)) for core in (0, 1) for i, j in around(n, way * (1 - 2 * core))]
                for way in (1, -1)
            ]
        )
    ahead = [lax.ppermute(v, g, w[0]) for v, g, w in zip(values, groups, ways)]
    behind = [lax.ppermute(v, g, w[1]) for v, g, w in zip(values, groups, ways)]
    across = [lax.ppermute(v, g, w[0]) for v, g, w in zip(ahead, groups, ways)]
    return [list(blocks) for blocks in zip(values, ahead, behind, across)]


def collect(value, axis, n):
    copies = jnp.broadcast_to(value[None], (n,) + value.shape)
    return lax.all_to_all(copies, axis, split_axis=0, concat_axis=0, tiled=True)


SHIFTS = (0, 1, 3, 2)
GROUP = 8


def weigh_kernel(owned, nz, place_ref, pattern_ref, weight_ref, block_ref, by_col_ref, by_chip_ref):
    lanes = 128
    row = place_ref[0]
    diagonal = lax.broadcasted_iota(jnp.int32, (owned, owned), 0) == lax.broadcasted_iota(
        jnp.int32, (owned, owned), 1
    )
    spread_weight = jnp.broadcast_to(weight_ref[...], (owned, owned))
    weight = jnp.sum(jnp.where(diagonal, spread_weight, 0.0), axis=1, keepdims=True)
    width = by_col_ref.shape[2]
    count = width // lanes
    chips, _, tile = by_chip_ref.shape
    half = tile // 2
    strips = []
    for z in range(nz):
        parts = []
        for i in range(count):
            j = z * count + i
            flag = pattern_ref[row, j].astype(jnp.float32)
            block = block_ref[:, j * lanes : (j + 1) * lanes].astype(jnp.float32)
            parts.append((block * weight * flag).astype(jnp.bfloat16))
        strip = jnp.concatenate(parts, 1)
        by_col_ref[z] = strip
        strips.append(strip)
    for x in range(4):
        for core in range(2):
            pair = jnp.concatenate(strips[x * 4 + core * 2 : x * 4 + core * 2 + 2], 1)
            for y in range(4):
                by_chip_ref[x * 4 + y, :, core * half : (core + 1) * half] = pair[
                    :, y * half : (y + 1) * half
                ]


def gram_kernel(half, steps, place_ref, rows_ref, *refs):
    x, y, c = place_ref[0], place_ref[1], place_ref[2]
    by_y, by_x, (keep_ref, send_ref, acc_ref) = refs[:4], refs[4:8], refs[8:]
    k = pl.program_id(0)
    way = 1 - 2 * c
    offsets = (0, way, -way, 2)

    def before(position, offset):
        return lax.rem(position - offset + 4, 4)

    def product(left, right):
        return lax.dot_general(
            jnp.concatenate(left, 0),
            jnp.concatenate(right, 0),
            (((0,), (0,)), ((), ())),
            preferred_element_type=jnp.float32,
        )

    def first():
        left, right = [], []
        for p in range(GROUP):
            for i in range(4):
                for j in range(4):
                    left.append(rows_ref[p, i * 4 + before(y, offsets[j])])
                    right.append(by_y[j][i, p])
        return product(left, right)

    def second():
        left, right = [], []
        for p in range(GROUP):
            for i in range(4):
                for j in range(4):
                    left.append(
                        rows_ref[p, before(x, offsets[i]) * 4 + before(y, SHIFTS[j])]
                    )
                    right.append(by_x[i][j, p])
        return product(left, right)

    @pl.when(k == 0)
    def _():
        acc_ref[...] = first()

    @pl.when(jnp.logical_and(k > 0, k < steps // 2))
    def _():
        acc_ref[...] += first()

    @pl.when(k >= steps // 2)
    def _():
        acc_ref[...] += second()

    last = k == steps - 1

    @pl.when(jnp.logical_and(last, c == 0))
    def _():
        keep_ref[...] = acc_ref[:half]
        send_ref[...] = acc_ref[half:]

    @pl.when(jnp.logical_and(last, c != 0))
    def _():
        keep_ref[...] = acc_ref[half:]
        send_ref[...] = acc_ref[:half]


def finish_kernel(factor, corner_ref, keep_ref, add_ref, out_ref, held_ref, sems):
    bands = held_ref.shape[0]
    rows, width = held_ref.shape[1:]
    copies = [
        pltpu.make_async_copy(keep_ref.at[pl.ds(i * rows, rows)], held_ref.at[i], sems.at[i])
        for i in range(bands)
    ]
    for copy in copies:
        copy.start()
    for i, copy in enumerate(copies):
        row_ids = corner_ref[0] + i * rows + lax.broadcasted_iota(jnp.int32, (rows, width), 0)
        col_ids = corner_ref[1] + lax.broadcasted_iota(jnp.int32, (rows, width), 1)
        copy.wait()
        total = (held_ref[i] + add_ref[i * rows : (i + 1) * rows]) * factor
        out_ref[i * rows : (i + 1) * rows] = jnp.where(
            row_ids == col_ids, jnp.float32(0.0), total
        ).astype(jnp.bfloat16)


def place_kernel(own_ref, ahead_ref, behind_ref, out_ref, sems):
    y = lax.axis_index("layer")
    way = 1 - 2 * lax.axis_index("core")
    copies = []
    for i, (ref, offset) in enumerate(((own_ref, 0), (ahead_ref, way), (behind_ref, -way))):
        slot = lax.rem(y - offset + 4, 4)
        copies.append(pltpu.make_async_copy(ref, out_ref.at[slot], sems.at[i]))
    for copy in copies:
        copy.start()
    for copy in copies:
        copy.wait()


def last_kernel(held_ref, across_ref, out_ref, sem):
    slot = lax.rem(lax.axis_index("layer") + 2, 4)
    copy = pltpu.make_async_copy(across_ref, out_ref.at[slot], sem)
    copy.start()
    copy.wait()


def assemble(own, ahead, behind, across):
    shape = jax.ShapeDtypeStruct((4,) + own.shape, own.dtype)
    params = pltpu.CompilerParams(vmem_limit_bytes=8 << 20)
    anywhere = pl.BlockSpec(memory_space=pl.ANY)
    held = pl.pallas_call(
        place_kernel,
        out_shape=shape,
        in_specs=[VMEM] * 3,
        out_specs=anywhere,
        scratch_shapes=[pltpu.SemaphoreType.DMA((3,))],
        compiler_params=params,
        name="place",
    )(own, ahead, behind)
    return pl.pallas_call(
        last_kernel,
        out_shape=shape,
        in_specs=[anywhere, VMEM],
        out_specs=anywhere,
        scratch_shapes=[pltpu.SemaphoreType.DMA],
        input_output_aliases={0: 0},
        compiler_params=params,
        name="last",
    )(held, across)


def body(occurrences, idf_weight, pattern):
    owned, reads = occurrences.shape
    nx, nc = lax.axis_size("x"), lax.axis_size("core")
    nz, ny = lax.axis_size("col"), lax.axis_size("layer")
    x, c = lax.axis_index("x"), lax.axis_index("core")
    z, y = lax.axis_index("col"), lax.axis_index("layer")
    factor = 1.0 / math.sqrt(owned * nx * nc * nz * ny)
    owner = lax.axis_index(("x", "core", "col", "layer"))
    width = reads // nz
    half = reads // (nx * nc * ny)
    tile = nc * half
    chips = nx * ny
    block_row = jnp.reshape(owner * owned // 128, (1,)).astype(jnp.int32)
    by_col, by_chip = pl.pallas_call(
        lambda *refs: weigh_kernel(owned, nz, *refs),
        out_shape=(
            jax.ShapeDtypeStruct((nz, owned, width), jnp.bfloat16),
            jax.ShapeDtypeStruct((chips, owned, tile), jnp.bfloat16),
        ),
        in_specs=[SMEM, SMEM, VMEM, VMEM],
        out_specs=(VMEM, VMEM),
        compiler_params=pltpu.CompilerParams(vmem_limit_bytes=58 << 20),
        name="weigh",
    )(block_row, pattern, idf_weight.reshape(1, owned), occurrences)
    own = lax.all_to_all(by_chip, ("x", "layer"), split_axis=0, concat_axis=0, tiled=True)
    own = own.reshape(chips * owned, tile)
    rows = lax.all_gather(own, "col", axis=0, tiled=True).reshape(nz, chips, owned, tile)
    by_col, own = lax.optimization_barrier((by_col, own))
    part = lax.all_to_all(by_col, "col", split_axis=0, concat_axis=0, tiled=True)
    upper, lower = part[: nz // 2], part[nz // 2 :]
    along_x = collect(upper, "x", nx)
    along_y = jnp.stack(spread(lower, "layer", ny))
    by_x, by_y = relay([along_y, along_x], ["x", "layer"], [nx, ny])

    place = jnp.stack([x, y, c]).astype(jnp.int32)
    steps = nz // GROUP
    n = steps // 2
    keep, send = pl.pallas_call(
        lambda *refs: gram_kernel(half, steps, *refs),
        out_shape=(jax.ShapeDtypeStruct((half, width), jnp.float32),) * 2,
        grid=(steps,),
        in_specs=[
            SMEM,
            pl.BlockSpec((GROUP, chips, owned, tile), lambda k: (k, 0, 0, 0)),
        ]
        + [
            pl.BlockSpec((nx, GROUP, owned, width), lambda k: (0, jnp.minimum(k, n - 1), 0, 0))
        ]
        * ny
        + [
            pl.BlockSpec((ny, GROUP, owned, width), lambda k: (0, jnp.maximum(k - n, 0), 0, 0))
        ]
        * nx,
        out_specs=(VMEM, VMEM),
        scratch_shapes=[pltpu.VMEM((tile, width), jnp.float32)],
        compiler_params=pltpu.CompilerParams(vmem_limit_bytes=52846592),
        cost_estimate=pl.CostEstimate(
            flops=2 * tile * width * nz * chips * owned,
            bytes_accessed=2 * (tile + width) * nz * chips * owned,
            transcendentals=0,
        ),
        name="gram",
    )(place, rows, *by_y, *by_x)
    add = lax.ppermute(send, "core", [(0, 1), (1, 0)])
    corner = jnp.stack([((x * nc + c) * ny + y) * half, z * width]).astype(jnp.int32)
    bands = 2
    piece = pl.pallas_call(
        lambda *refs: finish_kernel(factor, *refs),
        out_shape=jax.ShapeDtypeStruct((half, width), jnp.bfloat16),
        in_specs=[SMEM, pl.BlockSpec(memory_space=pl.ANY), VMEM],
        out_specs=VMEM,
        scratch_shapes=[
            pltpu.VMEM((bands, half // bands, width), jnp.float32),
            pltpu.SemaphoreType.DMA((bands,)),
        ],
        compiler_params=pltpu.CompilerParams(vmem_limit_bytes=16 << 20),
        name="finish",
    )(corner, keep, add)
    (pieces,) = relay([piece], ["layer"], [ny])
    return assemble(*pieces).reshape(ny * half, width)


def solution(mesh):
    rows, cols, layers = mesh.devices.shape
    fine = Mesh(mesh.devices.reshape(rows // 2, 2, cols, layers), ("x", "core", "col", "layer"))
    owners = ("x", "core", "col", "layer")
    return jax.shard_map(
        body,
        mesh=fine,
        in_specs=(P(owners, None), P(owners), P()),
        out_specs=P(("x", "core"), "col"),
        check_vma=False,
    )
```
